32 devices in a mesh: req: 8 (over z, x), tp: 4 (over y, core).
Axes of the slice: x: 2, y: 2, z: 4, core: 2. Of those that a mesh axis runs over, the one named last changes fastest.
Arguments:
- hidden_in: bfloat16 [8, 1024, 2048], P('req', None, 'tp'), may hold values from -6 to 6
- ln_gain: float32 [2048], replicated, may hold values from 0.25 to 1.75
- ln_bias: float32 [2048], replicated, may hold values from -1.5 to 1.5
- w_qkv: bfloat16 [3, 2048, 2048], P(None, None, 'tp'), may hold values from -0.125 to 0.125
- b_qkv: float32 [3, 2048], P(None, 'tp'), may hold values from -1.5 to 1.5
- w_out: bfloat16 [2048, 2048], P('tp'), may hold values from -0.125 to 0.125
- b_out: float32 [2048], replicated, may hold values from -1.5 to 1.5
- alibi_slope: float32 [16], P('tp'), may hold values from 2.4414063e-05 to 0.1
- prefix_k: bfloat16 [2048, 2048], P('req', 'tp'), may hold values from -160 to 160
- prefix_v: bfloat16 [2048, 2048], P('req', 'tp'), may hold values from -6 to 6
- suffix_len: int32 [8], P('req'), may hold values from 64 to 1024, as said below
- group_of: int32 [8], P('req'), may hold values from 0 to 1
- block_of_device: int32 [8], P('req'), may hold values from 0 to 7, each once
Outputs:
- mixed: bfloat16 [8, 1024, 2048], P('req', None, 'tp')
- cache_k: bfloat16 [8, 1024, 2048], P('req', None, 'tp')
- cache_v: bfloat16 [8, 1024, 2048], P('req', None, 'tp')
The draws below stay inside these ranges and needn't reach their ends.
Inputs may be any that keep to these rules, and one draw needn't show every extreme that they name: `suffix_len`: every request has at least 64 live slots; some request has exactly 1024.
All inputs are finite; a program needn't handle non-finite values.
Results may differ from the reference program's by a relative error of at most 0.011.
Values may be sent and summed in bfloat16 or wider, within the bound.
A program may use at most 384 MiB of HBM per device.

```python
import math
import jax
import jax.numpy as jnp
from jax import lax

D = 2048
H = 16
HD = 128
HH = 2048
SUF = 1024
PB = 256
REQS = 8
PREFIX = 1024
N_REQ = 8
N_TP = 4


def draw_suffix_len(key, part):
    first_key, second_key = jax.random.split(jax.random.fold_in(key, 11))
    lengths = jax.random.randint(first_key, (N_REQ,), SUF // 16, SUF + 1)
    chosen = jax.random.randint(second_key, (), 0, N_REQ)
    return jnp.where(jnp.arange(N_REQ) == chosen, SUF, lengths).astype(jnp.int32)


def draw_prefix_k(key, part):
    base = jax.random.normal(jax.random.fold_in(key, 23), (N_REQ * PB, HH), jnp.float32)
    base = jnp.clip(base, -6.0, 6.0)
    return jnp.clip(base, -160.0, 160.0).astype(jnp.bfloat16)


def plant(array, own_key, smallest, high):
    spot = [jax.random.randint(jax.random.fold_in(own_key, axis), (), 0, length) for axis, length in enumerate(array.shape)]
    widest = array.shape.index(max(array.shape))
    neighbour = spot[:widest] + [(spot[widest] + 1) % array.shape[widest]] + spot[widest + 1:]
    return array.at[tuple(spot)].set(smallest).at[tuple(neighbour)].set(high)


def levels(rng, extent, shards, least, high):
    def one(position, shards_of):
        steps = jax.random.uniform(jax.random.fold_in(jax.random.fold_in(rng, 6), position), (shards_of,), jnp.float32, least / len(shards), high / len(shards))
        return jnp.repeat(jnp.exp(steps), extent[position] // shards_of).reshape((-1,) + (1,) * (len(extent) - position - 1))

    level = one(*shards[0])
    for cut in shards[1:]:
        level = level * one(*cut)
    return level


def noise(key, shape, scale, bound, shards=(), held_as=jnp.bfloat16):
    level = levels(key, shape, shards, -0.22, 0.18) if shards else 1.0
    entries = jax.random.normal(key, shape, jnp.float32) * scale * level
    return jnp.minimum(jnp.maximum(entries, -bound), bound).astype(held_as)


def setup_inputs(seed: int = 0) -> dict:
    streams_of = jax.random.split(jax.random.key(seed), 14)
    return {
        "hidden_in": noise(streams_of[0], (REQS, SUF, D), 1.0, 6.0, ((0, 8), (2, 4))),
        "ln_gain": jnp.clip(1.0 + 0.15 * jax.random.normal(streams_of[1], (D,), jnp.float32), 0.25, 1.75),
        "ln_bias": noise(streams_of[2], (D,), 0.3, 1.5, (), jnp.float32),
        "w_qkv": noise(streams_of[3], (3, D, HH), D ** -0.5, 0.125, ((2, 4),)),
        "b_qkv": noise(streams_of[4], (3, HH), 0.3, 1.5, ((1, 4),), jnp.float32),
        "w_out": noise(streams_of[5], (HH, D), HH ** -0.5, 0.125, ((0, 4),)),
        "b_out": noise(streams_of[6], (D,), 0.3, 1.5, (), jnp.float32),
        "alibi_slope": jnp.clip(jnp.exp(math.log(0.1) - 8.317766 * jax.random.uniform(streams_of[7], (H,), jnp.float32) ** levels(streams_of[7], (H,), ((0, 4),), -0.2, 0.2)), 2.441406286379788e-05, 0.1),
        "prefix_k": draw_prefix_k(jax.random.fold_in(streams_of[13], 71), 0),
        "prefix_v": noise(streams_of[9], (N_REQ * PB, HH), 1.0, 6.0, ((0, 8), (1, 4))),
        "suffix_len": draw_suffix_len(jax.random.fold_in(streams_of[13], 71), 0),
        "group_of": plant(jax.random.randint(streams_of[11], (REQS,), 0, 2), jax.random.fold_in(streams_of[11], 1), 0, 1).astype(jnp.int32),
        "block_of_device": jax.random.permutation(streams_of[12], N_REQ).astype(jnp.int32),
    }


EPS = 1e-05
NEGATIVE = -1e+30

def reference(hidden_in, ln_gain, ln_bias, w_qkv, b_qkv, w_out, b_out, alibi_slope, prefix_k, prefix_v, suffix_len, group_of, block_of_device):
    holders = jnp.zeros((N_REQ,), jnp.int32).at[block_of_device].set(jnp.arange(N_REQ, dtype=jnp.int32))
    ordered_k = prefix_k.reshape(N_REQ, PB, HH)[holders].reshape(2, PREFIX, HH)
    ordered_v = prefix_v.reshape(N_REQ, PB, HH)[holders].reshape(2, PREFIX, HH)
    slot_ids = jnp.arange(SUF, dtype=jnp.int32)
    key_pos = jnp.concatenate([jnp.arange(PREFIX, dtype=jnp.int32), PREFIX + slot_ids])
    query_pos = PREFIX + slot_ids
    distance = (query_pos[:, None] - key_pos[None, :]).astype(jnp.float32)
    group_width = HH // N_TP
    out_groups = w_out.reshape(N_TP, group_width, D).astype(jnp.float32)

    def one_request(inputs):
        slot_rows, length, group = inputs
        values32 = slot_rows.astype(jnp.float32)
        center = values32 - lax.optimization_barrier(jnp.mean(values32, axis=1, keepdims=True))
        spread = lax.optimization_barrier(jnp.mean(center * center, axis=1, keepdims=True))
        normed = (center / jnp.sqrt(spread + EPS) * ln_gain + ln_bias).astype(jnp.bfloat16)
        projected = jnp.einsum('sd,cdh->csh', normed.astype(jnp.float32), w_qkv.astype(jnp.float32)) + b_qkv[:, None, :]
        projected = projected.astype(jnp.bfloat16)
        query, keys, values = (projected[0], projected[1], projected[2])
        live = slot_ids < length
        keys_out = jnp.where(live[:, None], keys, jnp.zeros_like(keys))
        values_out = jnp.where(live[:, None], values, jnp.zeros_like(values))
        all_keys = jnp.concatenate([ordered_k[group], keys], axis=0)
        all_values = jnp.concatenate([ordered_v[group], values], axis=0)
        allowed = (key_pos[None, :] < PREFIX) | (key_pos[None, :] <= query_pos[:, None]) & (key_pos[None, :] < PREFIX + length)
        query_heads = query.reshape(SUF, H, HD).astype(jnp.float32)
        key_heads = all_keys.reshape(PREFIX + SUF, H, HD).astype(jnp.float32)
        value_heads = all_values.reshape(PREFIX + SUF, H, HD).astype(jnp.float32)
        scores = jnp.einsum('shd,khd->hsk', query_heads, key_heads) / jnp.sqrt(jnp.float32(HD))
        scores = scores - alibi_slope[:, None, None] * distance[None, :, :]
        scores = jnp.where(allowed[None], scores, NEGATIVE)
        row_top = lax.optimization_barrier(jnp.max(scores, axis=2, keepdims=True))
        weights = jnp.where(allowed[None], jnp.exp(scores - row_top), 0.0)
        total = lax.optimization_barrier(jnp.sum(weights, axis=2))
        rounded = lax.optimization_barrier(weights.astype(jnp.bfloat16)).astype(jnp.float32)
        attended = jnp.einsum('hsk,khd->hsd', rounded, value_heads) / total[:, :, None]
        attended = attended.transpose(1, 0, 2).reshape(SUF, HH).astype(jnp.bfloat16)
        parts = attended.reshape(SUF, N_TP, group_width).astype(jnp.float32)
        partial_value = jnp.einsum('sgf,gfd->gsd', parts, out_groups)
        partial_value = lax.optimization_barrier(partial_value.astype(jnp.bfloat16)).astype(jnp.float32)
        result = lax.optimization_barrier(jnp.sum(partial_value, axis=0)) + b_out + values32
        result = jnp.where(live[:, None], result, 0.0).astype(jnp.bfloat16)
        return (result, keys_out, values_out)
    mixed, cache_k, cache_v = lax.map(one_request, (hidden_in, suffix_len, group_of))
    return (mixed, cache_k, cache_v)
```

```python
import functools
import math

import jax
import jax.numpy as jnp
from jax import lax
from jax.experimental import pallas as pl
from jax.experimental.pallas import tpu as pltpu
from jax.sharding import PartitionSpec as P

EPS = 1e-05
NEGATIVE = -1e30
LOG2E = math.log2(math.e)
ROWS = 256
STEP = 4
F32 = jnp.float32
BF16 = jnp.bfloat16


def dot_t(a, b):
    return lax.dot_general(a, b, (((1,), (1,)), ((), ())), preferred_element_type=F32)


def kernel(n_req, n_x, heads, *refs):
    (block_ref, group_ref, length_ref, slope, hid, gain_in, beta_in, w_qkv, b_qkv_in, w_out, b_out_in, pk, pv) = refs[:13]
    mixed, ck, cv = refs[13:16]
    (hbuf, wq, wcol, wst, nrm, qkv, cst, att, ost, gain, beta, b_qkv, b_out, ids, mine) = refs[16:31]
    kvh = refs[31 : 31 + heads]
    (loc, kvl, out_sem, hs, hr, zs, xs, es, kvr, as_, ar, wy_s, wy_r, wq_s, wq_r, ids_send, ids_recv) = refs[31 + heads :]

    slots, width = hid.shape[1], hid.shape[2]
    block = pk.shape[0]
    size = width // heads
    n_rc = slots // ROWS
    n_z = n_req // n_x
    nb = n_req // 2
    prefix = nb * block
    feats = 4 * width
    quarter = width // 4
    halved = tuple(h for h in range(heads) if h % 2 == 0)

    r = lax.axis_index("req")
    t = lax.axis_index("tp")
    y, c = t // 2, t % 2
    sib = y * 2 + (1 - c)
    oth = (1 - y) * 2 + c
    far = (1 - y) * 2 + (1 - c)
    z, x = r // n_x, r % n_x
    x_peers = [z * n_x + (x + d) % n_x for d in range(1, n_x)]
    z_even = z % 2 == 0
    z_pair = r + n_x - 2 * n_x * (z % 2)
    x_pair = r + 1 - 2 * (x % 2)
    quad = (z % 2) * 2 + x % 2
    quad_z = (1 - z % 2) * 2 + x % 2
    quad_x = (z % 2) * 2 + 1 - x % 2
    quad_d = (1 - z % 2) * 2 + 1 - x % 2

    def remote(src, dst, send, recv, dev):
        return pltpu.make_async_remote_copy(
            src_ref=src,
            dst_ref=dst,
            send_sem=send,
            recv_sem=recv,
            device_id=dev,
            device_id_type=pl.DeviceIdType.MESH,
        )

    def arrived(dst, recv):
        remote(dst, dst, loc.at[0], recv, (r, sib)).wait_recv()

    def rows_of(i):
        return pl.ds(pl.multiple_of(i * ROWS, ROWS), ROWS)

    def cols_of(k):
        return pl.ds(pl.multiple_of(k * width, width), width)

    def quarter_of(q):
        return pl.ds(pl.multiple_of(q * quarter, quarter), quarter)

    barrier = pltpu.get_barrier_semaphore()

    def greet(dev):
        pl.semaphore_signal(barrier, inc=1, device_id=dev, device_id_type=pl.DeviceIdType.MESH)

    greet((r, sib))
    greet((r, oth))

    def greet_req(d, carry):
        greet(((r + d) % n_req, t))
        return carry

    lax.fori_loop(1, n_req, greet_req, 0)

    def own_kv(h, a):
        cols = slice(h * size, (h + 1) * size)
        return pltpu.make_async_copy((pk, pv)[a].at[:, cols], kvh[h].at[r, a], kvl.at[h, a])

    own = [
        pltpu.make_async_copy(hid.at[0], hbuf.at[t], loc.at[0]),
        pltpu.make_async_copy(w_qkv, wq, loc.at[1]),
        pltpu.make_async_copy(w_out.at[:, cols_of(t)], wcol.at[t], loc.at[2]),
        pltpu.make_async_copy(gain_in, gain, loc.at[3]),
        pltpu.make_async_copy(beta_in, beta, loc.at[4]),
        pltpu.make_async_copy(b_qkv_in, b_qkv, loc.at[5]),
        pltpu.make_async_copy(b_out_in, b_out, loc.at[6]),
    ]
    for a in range(2):
        own_kv(0, a).start()
    for h in range(1, heads):
        for a in range(2):
            own_kv(h, a).start()
    for copy in own:
        copy.start()
    mine[...] = jnp.full(mine.shape, block_ref[0], jnp.int32)
    ids[r] = jnp.full(mine.shape, block_ref[0], jnp.int32)
    pl.semaphore_wait(barrier, n_req + 1)

    def h_other(i):
        rows = rows_of(i)
        return remote(hid.at[0, rows], hbuf.at[t, rows], hs.at[0, i], hr.at[0, i], (r, oth))

    def h_sib(i):
        rows = rows_of(i)
        return remote(hid.at[0, rows], hbuf.at[t, rows], hs.at[1, i], hr.at[1, i], (r, sib))

    def h_fwd(i):
        rows = rows_of(i)
        return remote(hbuf.at[oth, rows], hbuf.at[oth, rows], hs.at[2, i], hr.at[2, i], (r, sib))

    def w_sib():
        return remote(w_out.at[:, cols_of(sib)], wcol.at[t], wy_s.at[0], wy_r.at[0], (r, sib))

    def w_oth():
        rows = quarter_of(quad)
        return remote(w_out.at[rows, cols_of(oth)], wcol.at[t, rows], wy_s.at[1], wy_r.at[1], (r, oth))

    def w_far():
        rows = quarter_of(quad)
        return remote(w_out.at[rows, cols_of(far)], wst, wy_s.at[2], wy_r.at[2], (r, oth))

    def w_fwd():
        return remote(wst, wcol.at[oth, quarter_of(quad)], wy_s.at[3], wy_r.at[3], (r, sib))

    def w_piece(g, q, k, dev):
        here = wcol.at[(oth, far)[g], quarter_of(q)]
        return remote(here, here, wq_s.at[k], wq_r.at[k], (dev, t))

    def w_spread():
        return [w_piece(g, quad, k * 2 + g, (z_pair, x_pair)[k]) for k in range(2) for g in range(2)]

    def w_last():
        return [w_piece(0, quad_x, 4, z_pair), w_piece(1, quad_z, 5, x_pair)]

    def number(d):
        return remote(mine, ids.at[r], ids_send.at[d], ids_recv.at[r], ((r + d) % n_req, t))

    def up(h, zj):
        here = kvh[h].at[zj * n_x + x]
        return remote(here, here, zs.at[0, h, zj], kvr.at[h, zj * n_x + x], (r + n_x, t))

    def down(h, zj):
        here = kvh[h].at[zj * n_x + x]
        return remote(here, here, zs.at[1, h, zj], kvr.at[h, zj * n_x + x], (r - n_x, t))

    def across(h, zj, d):
        here = kvh[h].at[zj * n_x + x]
        return remote(here, here, xs.at[d, h, zj], kvr.at[h, zj * n_x + x], (x_peers[d], t))

    def extra(h, d):
        here = kvh[h].at[x_peers[d]]
        return remote(here, here, es.at[d, h], kvr.at[h, x_peers[d]], (z_pair, t))

    def kv_wait(h, j):
        arrived(kvh[h].at[j], kvr.at[h, j])

    def send_own(h):
        for a in range(2):
            own_kv(h, a).wait()

        @pl.when(z < n_z - 1)
        def _():
            up(h, z).start()

        @pl.when(z > 0)
        def _():
            down(h, z).start()

        for d in range(n_x - 1):
            across(h, z, d).start()

    def crosses(h, s, below):
        if h in halved and s == 1:
            return jnp.logical_not(z_even) if not below else z_even
        return None

    def pass_on(h, s):
        @pl.when(z - s >= 0)
        def _():
            zj = z - s
            kv_wait(h, zj * n_x + x)

            @pl.when(z < n_z - 1)
            def _():
                up(h, zj).start()

        @pl.when(z + s < n_z)
        def _():
            zj = z + s
            kv_wait(h, zj * n_x + x)

            @pl.when(z > 0)
            def _():
                down(h, zj).start()

        for below in (True, False):
            ok = (z - s >= 0) if below else (z + s < n_z)
            only = crosses(h, s, below)
            if only is not None:
                ok = jnp.logical_and(ok, only)

            @pl.when(ok)
            def _(below=below):
                for d in range(n_x - 1):
                    across(h, z - s if below else z + s, d).start()

        if h in halved and s == 1:
            for d in range(n_x - 1):
                kv_wait(h, x_peers[d])
                extra(h, d).start()

    def kv_rest(h):
        def one(zj, carry):
            def wait():
                for d in range(1, n_x):
                    kv_wait(h, zj * n_x + (x + d) % n_x)

            if h in halved:
                pl.when(zj != z)(wait)
            else:
                wait()
            return carry

        lax.fori_loop(0, n_z, one, 0)

    def tick(k):
        for h in range(heads):
            s = k - h
            if s == 0:
                send_own(h)
            elif 0 < s < n_z:
                pass_on(h, s)

    n_ticks = heads + n_z - 1

    h_other(0).start()
    h_sib(0).start()
    tick(0)
    for i in range(1, n_rc):
        h_other(i).start()
        h_sib(i).start()
    w_oth().start()
    w_far().start()
    w_sib().start()

    def send_number(d, carry):
        number(d).start()
        return carry

    lax.fori_loop(1, n_req, send_number, 0)
    tick(1)

    length = length_ref[0]

    def live(i):
        slot = lax.broadcasted_iota(jnp.int32, (ROWS, width), 0) + i * ROWS
        return slot < length

    def cache_out(i, j):
        rows = rows_of(i)
        dst = (ck, cv)[j]
        return pltpu.make_async_copy(cst.at[j, rows], dst.at[0, rows], out_sem.at[j, i])

    own[0].wait()
    for copy in own[3:]:
        copy.wait()
    own[1].wait()

    def project(i, carry):
        rows = rows_of(i)
        h_other(i).wait_recv()
        h_fwd(i).start()
        h_sib(i).wait_recv()
        h_fwd(i).wait_recv()
        pieces = [hbuf[f, rows, :].astype(F32) for f in range(4)]
        mean = sum(jnp.sum(p, axis=1, keepdims=True) for p in pieces) * (1.0 / feats)
        pieces = [p - mean for p in pieces]
        var = sum(jnp.sum(p * p, axis=1, keepdims=True) for p in pieces) * (1.0 / feats)
        inv = 1.0 / jnp.sqrt(var + EPS)
        for f in range(4):
            cols = slice(f * width, (f + 1) * width)
            nrm[:, cols] = (pieces[f] * inv * gain[:, cols] + beta[:, cols]).astype(BF16)
        keep = live(i)
        for j in range(3):
            out = jnp.dot(nrm[...], wq[j], preferred_element_type=F32) + b_qkv[j : j + 1, :]
            out = out.astype(BF16)
            for h in range(heads):
                qkv[j, h, rows, :] = out[:, h * size : (h + 1) * size]
            if j > 0:
                cst[j - 1, rows, :] = jnp.where(keep, out, jnp.zeros_like(out))
                cache_out(i, j - 1).start()
        for k in range(n_rc):
            if 2 + k < n_ticks and k < n_rc - 2:

                @pl.when(i == k)
                def _(k=k):
                    tick(2 + k)

        return carry

    lax.fori_loop(0, n_rc, project, 0)
    next_tick = 2 + max(0, n_rc - 2)

    def wait_number(d, carry):
        j = (r + d) % n_req
        arrived(ids.at[j], ids_recv.at[j])
        number(d).wait_send()
        return carry

    lax.fori_loop(1, n_req, wait_number, 0)
    first = group_ref[0] * nb

    def holder(p):
        found = jnp.zeros(mine.shape, jnp.int32)
        for j in range(n_req):
            found = jnp.maximum(found, jnp.where(ids[j] == first + p, j, 0))
        return jnp.max(found)

    holders = [holder(p) for p in range(nb)]

    scale2 = LOG2E / math.sqrt(size)
    tri = lax.broadcasted_iota(jnp.int32, (ROWS, ROWS), 1) <= lax.broadcasted_iota(
        jnp.int32, (ROWS, ROWS), 0
    )
    slot_ids = lax.broadcasted_iota(jnp.int32, (1, slots), 1)
    block_ids = lax.broadcasted_iota(jnp.int32, (1, block), 1)

    def a_other(h, i):
        here = att.at[t, rows_of(i), h * size : (h + 1) * size]
        return remote(here, here, as_.at[0, h, i], ar.at[0, h, i], (r, oth))

    def a_sib(h, i):
        here = att.at[t, rows_of(i), h * size : (h + 1) * size]
        return remote(here, here, as_.at[1, h, i], ar.at[1, h, i], (r, sib))

    def a_fwd(h, i):
        here = att.at[oth, rows_of(i), h * size : (h + 1) * size]
        return remote(here, here, as_.at[2, h, i], ar.at[2, h, i], (r, sib))

    def attend(h, i):
        lo, hi = i * ROWS, (i + 1) * ROWS
        slope2 = slope[h] * LOG2E
        q = qkv[0, h, lo:hi, :]
        shift = jnp.where(slot_ids < length, slot_ids.astype(F32) * slope2, NEGATIVE)
        sd = dot_t(q, qkv[1, h, lo:hi, :]) * scale2 + shift[:, lo:hi]
        scores = [(jnp.where(tri, sd, NEGATIVE), lambda: qkv[2, h, lo:hi, :])]
        if i > 0:
            so = dot_t(q, qkv[1, h, 0:lo, :]) * scale2 + shift[:, 0:lo]
            scores.append((so, lambda: qkv[2, h, 0:lo, :]))

        def part(p, j):
            place = (block_ids + (p * block - prefix)).astype(F32) * slope2
            return dot_t(q, kvh[h][j, 0]) * scale2 + place, lambda: kvh[h][j, 1]

        def fold(scores, state):
            m = state[0] if state else None
            for s, _ in scores:
                top = jnp.max(s, axis=1, keepdims=True)
                m = top if m is None else jnp.maximum(m, top)
            total = out = None
            if state:
                fac = jnp.exp2(state[0] - m)
                total, out = state[1] * fac, state[2] * fac
            for s, values in scores:
                w = jnp.exp2(s - m)
                sums = jnp.sum(w, axis=1, keepdims=True)
                prod = jnp.dot(w.astype(BF16), values(), preferred_element_type=F32)
                total = sums if total is None else total + sums
                out = prod if out is None else out + prod
            return m, total, out

        state = None
        for g in range(nb // STEP):
            scores += [part(g * STEP + k, holders[g * STEP + k]) for k in range(STEP)]
            state = fold(scores, state)
            scores = []
        att[t, lo:hi, h * size : (h + 1) * size] = (state[2] / state[1]).astype(BF16)
        a_other(h, i).start()
        a_sib(h, i).start()

    def weights_first():
        arrived(wst, wy_r.at[2])
        w_fwd().start()

    def weights_spread():
        here = quarter_of(quad)
        arrived(wcol.at[oth, here], wy_r.at[1])
        arrived(wcol.at[far, here], wy_r.at[3])
        for copy in w_spread():
            copy.start()

    def weights_last():
        arrived(wcol.at[oth, quarter_of(quad_x)], wq_r.at[2])
        arrived(wcol.at[far, quarter_of(quad_z)], wq_r.at[1])
        for copy in w_last():
            copy.start()

    def weights_rest():
        own[2].wait()
        arrived(wcol.at[sib], wy_r.at[0])
        arrived(wcol.at[oth, quarter_of(quad_z)], wq_r.at[0])
        arrived(wcol.at[far, quarter_of(quad_x)], wq_r.at[3])
        arrived(wcol.at[oth, quarter_of(quad_d)], wq_r.at[4])
        arrived(wcol.at[far, quarter_of(quad_d)], wq_r.at[5])

    events = {0: [next_tick], n_rc: [next_tick + 1], 2 * n_rc: [next_tick + 2]}
    other = {n_rc + 2: weights_first, n_rc + 3: weights_spread, 3 * n_rc + 2: weights_last}
    for h in range(heads):
        for i in range(n_rc):
            unit = h * n_rc + i
            due = events.get(unit, [])
            due = [k for k in due if k < n_ticks]
            if i == 0:
                due = sorted(set(due) | set(range(next_tick, h + n_z)))
            for k in due:
                if k >= next_tick:
                    for j in range(next_tick, k + 1):
                        tick(j)
                    next_tick = k + 1
            if unit in other:
                other[unit]()
            if i == 0:
                kv_rest(h)
            attend(h, i)

    def a_take(h, i):
        arrived(att.at[oth, rows_of(i), h * size : (h + 1) * size], ar.at[0, h, i])
        a_fwd(h, i).start()

    for h in range(heads - 1):

        def take(i, carry, h=h):
            a_take(h, i)
            return carry

        lax.fori_loop(0, n_rc, take, 0)
    weights_rest()

    def mixed_out(i):
        rows = rows_of(i)
        return pltpu.make_async_copy(ost.at[rows], mixed.at[0, rows], out_sem.at[2, i])

    def final(i, carry):
        rows = rows_of(i)

        def term(f):
            return jnp.dot(att[f, rows, :], wcol[f], preferred_element_type=F32)

        for h in range(heads):
            arrived(att.at[sib, rows, h * size : (h + 1) * size], ar.at[1, h, i])
        out = term(t) + term(sib)
        a_take(heads - 1, i)
        out = out + term(oth)
        for h in range(heads):
            arrived(att.at[far, rows, h * size : (h + 1) * size], ar.at[2, h, i])
        out = out + term(far)
        out = out + b_out[t] + hbuf[t, rows, :].astype(F32)
        ost[rows, :] = jnp.where(live(i), out, 0.0).astype(BF16)
        mixed_out(i).start()
        return carry

    lax.fori_loop(0, n_rc, final, 0)

    def drain(i, carry):
        h_other(i).wait_send()
        h_sib(i).wait_send()
        h_fwd(i).wait_send()
        for h in range(heads):
            a_other(h, i).wait_send()
            a_sib(h, i).wait_send()
            a_fwd(h, i).wait_send()
        cache_out(i, 0).wait()
        cache_out(i, 1).wait()
        return carry

    lax.fori_loop(0, n_rc, drain, 0)
    for copy in [w_sib(), w_oth(), w_far(), w_fwd()] + w_spread() + w_last():
        copy.wait_send()

    def drain_prefix(zj, carry):
        for h in range(heads):

            @pl.when(jnp.logical_and(zj <= z, z < n_z - 1))
            def _(h=h):
                up(h, zj).wait_send()

            @pl.when(jnp.logical_and(zj >= z, z > 0))
            def _(h=h):
                down(h, zj).wait_send()

            def waits(h=h):
                for d in range(n_x - 1):
                    across(h, zj, d).wait_send()

            if h in halved:
                pl.when(zj != z + 1 - 2 * (z % 2))(waits)
            else:
                waits()
        return carry

    lax.fori_loop(0, n_z, drain_prefix, 0)
    for h in halved:
        for d in range(n_x - 1):
            extra(h, d).wait_send()

    def drain_out(i, carry):
        mixed_out(i).wait()
        return carry

    lax.fori_loop(0, n_rc, drain_out, 0)


def on_device(
    n_req,
    n_x,
    hidden_in,
    ln_gain,
    ln_bias,
    w_qkv,
    b_qkv,
    w_out,
    b_out,
    alibi_slope,
    prefix_k,
    prefix_v,
    suffix_len,
    group_of,
    block_of_device,
):
    _, slots, width = hidden_in.shape
    heads = alibi_slope.shape[0]
    size = w_qkv.shape[2] // heads
    block = prefix_k.shape[0]
    n_rc = slots // ROWS
    n_z = n_req // n_x
    smem = pl.BlockSpec(memory_space=pltpu.SMEM)
    anywhere = pl.BlockSpec(memory_space=pl.ANY)
    dma = pltpu.SemaphoreType.DMA
    cache = jax.ShapeDtypeStruct((1, slots, width), BF16)
    return pl.pallas_call(
        functools.partial(kernel, n_req, n_x, heads),
        out_shape=(cache, cache, cache),
        in_specs=[smem] * 4 + [anywhere] * 9,
        out_specs=(anywhere, anywhere, anywhere),
        scratch_shapes=[
            pltpu.VMEM((4, slots, width), BF16),
            pltpu.VMEM(w_qkv.shape, BF16),
            pltpu.VMEM((4, w_out.shape[0], width), BF16),
            pltpu.VMEM((w_out.shape[0] // 4, width), BF16),
            pltpu.VMEM((ROWS, 4 * width), BF16),
            pltpu.VMEM((3, heads, slots, size), BF16),
            pltpu.VMEM((2, slots, width), BF16),
            pltpu.VMEM((4, slots, width), BF16),
            pltpu.VMEM((slots, width), BF16),
            pltpu.VMEM((1, 4 * width), F32),
            pltpu.VMEM((1, 4 * width), F32),
            pltpu.VMEM((3, width), F32),
            pltpu.VMEM((4, 1, width), F32),
            pltpu.VMEM((n_req, 8, 128), jnp.int32),
            pltpu.VMEM((8, 128), jnp.int32),
        ]
        + [pltpu.VMEM((n_req, 2, block, size), BF16) for _ in range(heads)]
        + [
            dma((7,)),
            dma((heads, 2)),
            dma((3, n_rc)),
            dma((3, n_rc)),
            dma((3, n_rc)),
            dma((2, heads, n_z)),
            dma((n_x - 1, heads, n_z)),
            dma((n_x - 1, heads)),
            dma((heads, n_req)),
            dma((3, heads, n_rc)),
            dma((3, heads, n_rc)),
            dma((4,)),
            dma((4,)),
            dma((6,)),
            dma((6,)),
            dma((n_req,)),
            dma((n_req,)),
        ],
        compiler_params=pltpu.CompilerParams(
            collective_id=0, has_side_effects=True, vmem_limit_bytes=60 << 20
        ),
        name="sublayer",
    )(
        block_of_device,
        group_of,
        suffix_len,
        alibi_slope,
        hidden_in,
        ln_gain[None],
        ln_bias[None],
        w_qkv,
        b_qkv,
        w_out,
        b_out.reshape(4, 1, width),
        prefix_k,
        prefix_v,
    )


def solution(mesh):
    n_req = mesh.shape["req"]
    n_x = 2 if n_req <= 8 else 4
    return jax.shard_map(
        functools.partial(on_device, n_req, n_x),
        mesh=mesh,
        in_specs=(
            P("req", None, "tp"),
            P(),
            P(),
            P(None, None, "tp"),
            P(None, "tp"),
            P("tp", None),
            P(),
            P("tp"),
            P("req", "tp"),
            P("req", "tp"),
            P("req"),
            P("req"),
            P("req"),
        ),
        out_specs=(P("req", None, "tp"), P("req", None, "tp"), P("req", None, "tp")),
        check_vma=False,
    )
```

```python
import functools
import math

import jax
import jax.numpy as jnp
from jax import lax
from jax.experimental import pallas as pl
from jax.experimental.pallas import tpu as pltpu
from jax.sharding import PartitionSpec as P

EPS = 1e-05
NEGATIVE = -1e30
LOG2E = math.log2(math.e)
ROWS = 256
STEP = 4
F32 = jnp.float32
BF16 = jnp.bfloat16


def dot_t(a, b):
    return lax.dot_general(a, b, (((1,), (1,)), ((), ())), preferred_element_type=F32)


PLAN = (
    ("own", 2), ("hidden", 0), ("own", 0), ("hidden", 1), ("below", 2, 1), ("hidden", 2), ("above", 2, 1),
    ("below", 0, 1), ("above", 0, 1), ("own", 1), ("project", 0), ("below", 2, 2), ("hidden", 3),
    ("weights",), ("above", 2, 2), ("project", 1), ("above", 0, 2), ("above", 2, 3), ("below", 0, 2),
    ("below", 2, 3), ("own", 3), ("below", 1, 1), ("project", 2), ("above", 1, 1), ("below", 0, 3),
    ("below", 3, 1), ("above", 3, 1), ("above", 0, 3), ("project", 3), ("above", 1, 2), ("below", 1, 2),
    ("attend", 2, 0), ("attend", 2, 3), ("above", 3, 2), ("below", 3, 2), ("attend", 0, 2), ("attend", 0, 3),
    ("w1",), ("peer", 1), ("attend", 0, 1), ("below", 1, 3), ("above", 1, 3), ("attend", 0, 0), ("peer", 3),
    ("below", 3, 3), ("attend", 2, 2), ("attend", 2, 1), ("above", 3, 3), ("w2",), ("attend", 1, 0),
    ("attend", 1, 3), ("attend", 1, 1), ("attend", 1, 2), ("attend", 3, 0), ("attend", 3, 1),
    ("attend", 3, 2), ("attend", 3, 3), ("w3",), ("w4",),
)
HALVED = (1, 3)


def plan(heads, n_rc, n_z):
    if (heads, n_rc, n_z) == (4, 4, 4):
        return PLAN
    steps = [("hidden", i) for i in range(n_rc)] + [("weights",)]
    for k in range(heads + n_z - 1):
        for h in range(heads):
            s = k - h
            if s == 0:
                steps.append(("own", h))
            elif 0 < s < n_z:
                steps += [("below", h, s), ("above", h, s)]
                if s == 1 and h in HALVED:
                    steps.append(("peer", h))
        if 0 < k <= n_rc:
            steps.append(("project", k - 1))
    steps += [("w1",), ("w2",), ("w3",), ("w4",)]
    return steps + [("attend", h, i) for h in range(heads) for i in range(n_rc)]


def kernel(n_req, n_x, heads, *refs):
    (block_ref, group_ref, length_ref, slope, hid, gain_in, beta_in, w_qkv, b_qkv_in, w_out, b_out_in, pk, pv) = refs[:13]
    mixed, ck, cv = refs[13:16]
    (hbuf, wq, wcol, wst, nrm, qkv, att, acc, gain, beta, b_qkv, b_out, ids, mine) = refs[16:30]
    kvh = refs[30 : 30 + heads]
    (loc, kvl, hs, hr, zs, xs, es, kvr, as_, ar, wy_s, wy_r, wq_s, wq_r, ids_send, ids_recv) = refs[30 + heads :]

    slots, width = hid.shape[1], hid.shape[2]
    block = pk.shape[0]
    size = width // heads
    n_rc = slots // ROWS
    n_z = n_req // n_x
    nb = n_req // 2
    prefix = nb * block
    feats = 4 * width
    quarter = width // 4

    r = lax.axis_index("req")
    t = lax.axis_index("tp")
    y, c = t // 2, t % 2
    sib = y * 2 + (1 - c)
    oth = (1 - y) * 2 + c
    far = (1 - y) * 2 + (1 - c)
    z, x = r // n_x, r % n_x
    x_peers = [z * n_x + (x + d) % n_x for d in range(1, n_x)]
    z_even = z % 2 == 0
    z_pair = r + n_x - 2 * n_x * (z % 2)
    x_pair = r + 1 - 2 * (x % 2)
    quad = (z % 2) * 2 + x % 2
    quad_z = (1 - z % 2) * 2 + x % 2
    quad_x = (z % 2) * 2 + 1 - x % 2
    quad_d = (1 - z % 2) * 2 + 1 - x % 2

    def remote(src, dst, send, recv, dev):
        return pltpu.make_async_remote_copy(
            src_ref=src,
            dst_ref=dst,
            send_sem=send,
            recv_sem=recv,
            device_id=dev,
            device_id_type=pl.DeviceIdType.MESH,
        )

    def arrived(dst, recv):
        remote(dst, dst, loc.at[0], recv, (r, sib)).wait_recv()

    def rows_of(i):
        return pl.ds(pl.multiple_of(i * ROWS, ROWS), ROWS)

    def cols_of(k):
        return pl.ds(pl.multiple_of(k * width, width), width)

    def quarter_of(q):
        return pl.ds(pl.multiple_of(q * quarter, quarter), quarter)

    barrier = pltpu.get_barrier_semaphore()

    def greet(dev):
        pl.semaphore_signal(barrier, inc=1, device_id=dev, device_id_type=pl.DeviceIdType.MESH)

    greet((r, sib))
    greet((r, oth))

    def greet_req(d, carry):
        greet(((r + d) % n_req, t))
        return carry

    lax.fori_loop(1, n_req, greet_req, 0)

    def own_kv(h, a):
        cols = slice(h * size, (h + 1) * size)
        return pltpu.make_async_copy((pk, pv)[a].at[:, cols], kvh[h].at[r, a], kvl.at[h, a])

    own = [
        pltpu.make_async_copy(hid.at[0], hbuf.at[t], loc.at[0]),
        pltpu.make_async_copy(w_qkv, wq, loc.at[1]),
        pltpu.make_async_copy(w_out.at[:, cols_of(t)], wcol.at[t], loc.at[2]),
        pltpu.make_async_copy(gain_in, gain, loc.at[3]),
        pltpu.make_async_copy(beta_in, beta, loc.at[4]),
        pltpu.make_async_copy(b_qkv_in, b_qkv, loc.at[5]),
        pltpu.make_async_copy(b_out_in, b_out, loc.at[6]),
    ]
    for a in range(2):
        own_kv(0, a).start()
    for h in range(1, heads):
        for a in range(2):
            own_kv(h, a).start()
    for copy in own:
        copy.start()
    mine[...] = jnp.full(mine.shape, block_ref[0], jnp.int32)
    ids[r] = jnp.full(mine.shape, block_ref[0], jnp.int32)
    pl.semaphore_wait(barrier, n_req + 1)

    def h_other(i):
        rows = rows_of(i)
        return remote(hid.at[0, rows], hbuf.at[t, rows], hs.at[0, i], hr.at[0, i], (r, oth))

    def h_sib(i):
        rows = rows_of(i)
        return remote(hid.at[0, rows], hbuf.at[t, rows], hs.at[1, i], hr.at[1, i], (r, sib))

    def h_fwd(i):
        rows = rows_of(i)
        return remote(hbuf.at[oth, rows], hbuf.at[oth, rows], hs.at[2, i], hr.at[2, i], (r, sib))

    def w_sib():
        return remote(w_out.at[:, cols_of(sib)], wcol.at[t], wy_s.at[0], wy_r.at[0], (r, sib))

    def w_oth():
        rows = quarter_of(quad)
        return remote(w_out.at[rows, cols_of(oth)], wcol.at[t, rows], wy_s.at[1], wy_r.at[1], (r, oth))

    def w_far():
        rows = quarter_of(quad)
        return remote(w_out.at[rows, cols_of(far)], wst, wy_s.at[2], wy_r.at[2], (r, oth))

    def w_fwd():
        return remote(wst, wcol.at[oth, quarter_of(quad)], wy_s.at[3], wy_r.at[3], (r, sib))

    def w_piece(g, q, k, dev):
        here = wcol.at[(oth, far)[g], quarter_of(q)]
        return remote(here, here, wq_s.at[k], wq_r.at[k], (dev, t))

    def w_spread():
        return [w_piece(g, quad, k * 2 + g, (z_pair, x_pair)[k]) for k in range(2) for g in range(2)]

    def w_last(k):
        return w_piece(k, (quad_x, quad_z)[k], 4 + k, (z_pair, x_pair)[k])

    def number(d):
        return remote(mine, ids.at[r], ids_send.at[d], ids_recv.at[r], ((r + d) % n_req, t))

    def up(h, zj):
        here = kvh[h].at[zj * n_x + x]
        return remote(here, here, zs.at[0, h, zj], kvr.at[h, zj * n_x + x], (r + n_x, t))

    def down(h, zj):
        here = kvh[h].at[zj * n_x + x]
        return remote(here, here, zs.at[1, h, zj], kvr.at[h, zj * n_x + x], (r - n_x, t))

    def across(h, zj, d):
        here = kvh[h].at[zj * n_x + x]
        return remote(here, here, xs.at[d, h, zj], kvr.at[h, zj * n_x + x], (x_peers[d], t))

    def extra(h, d):
        here = kvh[h].at[x_peers[d]]
        return remote(here, here, es.at[d, h], kvr.at[h, x_peers[d]], (z_pair, t))

    def kv_wait(h, j):
        arrived(kvh[h].at[j], kvr.at[h, j])

    def send_own(h):
        for a in range(2):
            own_kv(h, a).wait()

        @pl.when(z < n_z - 1)
        def _():
            up(h, z).start()

        @pl.when(z > 0)
        def _():
            down(h, z).start()

        for d in range(n_x - 1):
            across(h, z, d).start()

    def from_below(h, s):
        @pl.when(z - s >= 0)
        def _():
            zj = z - s
            kv_wait(h, zj * n_x + x)

            @pl.when(z < n_z - 1)
            def _():
                up(h, zj).start()

            spread(h, s, zj, z_even)

    def from_above(h, s):
        @pl.when(z + s < n_z)
        def _():
            zj = z + s
            kv_wait(h, zj * n_x + x)

            @pl.when(z > 0)
            def _():
                down(h, zj).start()

            spread(h, s, zj, jnp.logical_not(z_even))

    def spread(h, s, zj, whole):
        def go():
            for d in range(n_x - 1):
                across(h, zj, d).start()

        if h in HALVED and s == 1:
            pl.when(whole)(go)
        else:
            go()

    def pass_peer(h):
        for d in range(n_x - 1):
            kv_wait(h, x_peers[d])
            extra(h, d).start()

    def kv_rest(h):
        def one(zj, carry):
            def wait():
                for d in range(1, n_x):
                    kv_wait(h, zj * n_x + (x + d) % n_x)

            if h in HALVED:
                pl.when(zj != z)(wait)
            else:
                wait()
            return carry

        lax.fori_loop(0, n_z, one, 0)

    length = length_ref[0]

    def live(i):
        slot = lax.broadcasted_iota(jnp.int32, (ROWS, width), 0) + i * ROWS
        return slot < length

    def project(i):
        rows = rows_of(i)
        h_other(i).wait_recv()
        h_fwd(i).start()
        h_sib(i).wait_recv()
        h_fwd(i).wait_recv()
        pieces = [hbuf[f, rows, :].astype(F32) for f in range(4)]
        mean = sum(jnp.sum(p, axis=1, keepdims=True) for p in pieces) * (1.0 / feats)
        pieces = [p - mean for p in pieces]
        var = sum(jnp.sum(p * p, axis=1, keepdims=True) for p in pieces) * (1.0 / feats)
        inv = 1.0 / jnp.sqrt(var + EPS)
        for f in range(4):
            cols = slice(f * width, (f + 1) * width)
            nrm[:, cols] = (pieces[f] * inv * gain[:, cols] + beta[:, cols]).astype(BF16)
        keep = live(i)
        for j in range(3):
            out = jnp.dot(nrm[...], wq[j], preferred_element_type=F32) + b_qkv[j : j + 1, :]
            out = out.astype(BF16)
            for h in range(heads):
                qkv[j, h, rows, :] = out[:, h * size : (h + 1) * size]
            if j > 0:
                (ck, cv)[j - 1][0, rows, :] = jnp.where(keep, out, jnp.zeros_like(out))

    scale2 = LOG2E / math.sqrt(size)
    tri = lax.broadcasted_iota(jnp.int32, (ROWS, ROWS), 1) <= lax.broadcasted_iota(
        jnp.int32, (ROWS, ROWS), 0
    )
    slot_ids = lax.broadcasted_iota(jnp.int32, (1, slots), 1)
    block_ids = lax.broadcasted_iota(jnp.int32, (1, block), 1)

    def a_other(h, i):
        here = att.at[t, h, rows_of(i)]
        return remote(here, here, as_.at[0, h, i], ar.at[0, h, i], (r, oth))

    def a_sib(h, i):
        here = att.at[t, h, rows_of(i)]
        return remote(here, here, as_.at[1, h, i], ar.at[1, h, i], (r, sib))

    def a_fwd(h, i):
        here = att.at[oth, h, rows_of(i)]
        return remote(here, here, as_.at[2, h, i], ar.at[2, h, i], (r, sib))

    def attend(h, i):
        lo, hi = i * ROWS, (i + 1) * ROWS
        slope2 = slope[h] * LOG2E
        q = qkv[0, h, lo:hi, :]
        shift = jnp.where(slot_ids < length, slot_ids.astype(F32) * slope2, NEGATIVE)
        sd = dot_t(q, qkv[1, h, lo:hi, :]) * scale2 + shift[:, lo:hi]
        scores = [(jnp.where(tri, sd, NEGATIVE), lambda: qkv[2, h, lo:hi, :])]
        if i > 0:
            so = dot_t(q, qkv[1, h, 0:lo, :]) * scale2 + shift[:, 0:lo]
            scores.append((so, lambda: qkv[2, h, 0:lo, :]))

        def part(p, j):
            place = (block_ids + (p * block - prefix)).astype(F32) * slope2
            return dot_t(q, kvh[h][j, 0]) * scale2 + place, lambda: kvh[h][j, 1]

        def fold(scores, state):
            m = state[0] if state else None
            for s, _ in scores:
                top = jnp.max(s, axis=1, keepdims=True)
                m = top if m is None else jnp.maximum(m, top)
            total = out = None
            if state:
                fac = jnp.exp2(state[0] - m)
                total, out = state[1] * fac, state[2] * fac
            for s, values in scores:
                w = jnp.exp2(s - m)
                sums = jnp.sum(w, axis=1, keepdims=True)
                prod = jnp.dot(w.astype(BF16), values(), preferred_element_type=F32)
                total = sums if total is None else total + sums
                out = prod if out is None else out + prod
            return m, total, out

        state = None
        for g in range(nb // STEP):
            scores += [part(g * STEP + k, holders[g * STEP + k]) for k in range(STEP)]
            state = fold(scores, state)
            scores = []
        att[t, h, lo:hi, :] = (state[2] / state[1]).astype(BF16)
        a_other(h, i).start()
        a_sib(h, i).start()

    def weights_first():
        arrived(wst, wy_r.at[2])
        w_fwd().start()

    def weights_spread():
        here = quarter_of(quad)
        arrived(wcol.at[oth, here], wy_r.at[1])
        arrived(wcol.at[far, here], wy_r.at[3])
        for copy in w_spread():
            copy.start()

    def weights_third():
        arrived(wcol.at[oth, quarter_of(quad_x)], wq_r.at[2])
        w_last(0).start()

    def weights_fourth():
        arrived(wcol.at[far, quarter_of(quad_z)], wq_r.at[1])
        w_last(1).start()

    def weights_rest():
        own[2].wait()
        arrived(wcol.at[sib], wy_r.at[0])
        arrived(wcol.at[oth, quarter_of(quad_z)], wq_r.at[0])
        arrived(wcol.at[far, quarter_of(quad_x)], wq_r.at[3])
        arrived(wcol.at[oth, quarter_of(quad_d)], wq_r.at[4])
        arrived(wcol.at[far, quarter_of(quad_d)], wq_r.at[5])

    def hidden_send(i):
        h_other(i).start()
        h_sib(i).start()

    def weights_send():
        w_oth().start()
        w_far().start()
        w_sib().start()

    begun = set()

    def attend_unit(h, i):
        if h not in begun:
            begun.add(h)
            kv_rest(h)
        attend(h, i)

    do = {
        "hidden": hidden_send,
        "weights": weights_send,
        "own": send_own,
        "below": from_below,
        "above": from_above,
        "peer": pass_peer,
        "w1": weights_first,
        "w2": weights_spread,
        "w3": weights_third,
        "w4": weights_fourth,
        "attend": attend_unit,
    }
    groups = [[]]
    for step in plan(heads, n_rc, n_z):
        if step[0] == "project":
            groups.append([])
        else:
            groups[-1].append(step)

    def run(steps):
        for step in steps:
            do[step[0]](*step[1:])

    def send_number(d, carry):
        number(d).start()
        return carry

    lax.fori_loop(1, n_req, send_number, 0)
    run(groups[0])

    def wait_number(d, carry):
        j = (r + d) % n_req
        arrived(ids.at[j], ids_recv.at[j])
        number(d).wait_send()
        return carry

    lax.fori_loop(1, n_req, wait_number, 0)
    first = group_ref[0] * nb

    def holder(p):
        found = jnp.zeros(mine.shape, jnp.int32)
        for j in range(n_req):
            found = jnp.maximum(found, jnp.where(ids[j] == first + p, j, 0))
        return jnp.max(found)

    holders = [holder(p) for p in range(nb)]
    own[0].wait()
    for copy in own[3:]:
        copy.wait()
    own[1].wait()

    def prepare(i, carry):
        project(i)
        for k in range(n_rc - 1):
            if groups[k + 1]:

                @pl.when(i == k)
                def _(k=k):
                    run(groups[k + 1])

        return carry

    lax.fori_loop(0, n_rc, prepare, 0)
    run(groups[n_rc])

    def a_take(h, i):
        arrived(att.at[oth, h, rows_of(i)], ar.at[0, h, i])
        a_fwd(h, i).start()

    for h in range(heads - 1):

        def take(i, carry, h=h):
            a_take(h, i)
            return carry

        lax.fori_loop(0, n_rc, take, 0)
    weights_rest()

    a_take(heads - 1, 0)

    def final(i, carry):
        rows = rows_of(i)

        def term(f):
            lhs = jnp.concatenate([att[f, h, rows, :] for h in range(heads)], axis=1)
            return jnp.dot(lhs, wcol[f], preferred_element_type=F32)

        for h in range(heads):
            arrived(att.at[sib, h, rows], ar.at[1, h, i])
        acc[...] = term(t) + term(sib) + term(oth) + b_out[t] + hbuf[t, rows, :].astype(F32)

        @pl.when(i + 1 < n_rc)
        def _():
            a_take(heads - 1, i + 1)

        for h in range(heads):
            arrived(att.at[far, h, rows], ar.at[2, h, i])
        out = acc[...] + term(far)
        mixed[0, rows, :] = jnp.where(live(i), out, 0.0).astype(BF16)
        return carry

    lax.fori_loop(0, n_rc, final, 0)

    def drain(i, carry):
        h_other(i).wait_send()
        h_sib(i).wait_send()
        h_fwd(i).wait_send()
        for h in range(heads):
            a_other(h, i).wait_send()
            a_sib(h, i).wait_send()
            a_fwd(h, i).wait_send()
        return carry

    lax.fori_loop(0, n_rc, drain, 0)
    for copy in [w_sib(), w_oth(), w_far(), w_fwd()] + w_spread() + [w_last(0), w_last(1)]:
        copy.wait_send()

    def drain_prefix(zj, carry):
        for h in range(heads):

            @pl.when(jnp.logical_and(zj <= z, z < n_z - 1))
            def _(h=h):
                up(h, zj).wait_send()

            @pl.when(jnp.logical_and(zj >= z, z > 0))
            def _(h=h):
                down(h, zj).wait_send()

            def waits(h=h):
                for d in range(n_x - 1):
                    across(h, zj, d).wait_send()

            if h in HALVED:
                pl.when(zj != z + 1 - 2 * (z % 2))(waits)
            else:
                waits()
        return carry

    lax.fori_loop(0, n_z, drain_prefix, 0)
    for h in HALVED:
        for d in range(n_x - 1):
            extra(h, d).wait_send()


def land(*refs):
    copies = [pltpu.make_async_copy(refs[k], refs[k + 3], refs[6].at[k]) for k in range(3)]
    for copy in copies:
        copy.start()
    for copy in copies:
        copy.wait()


def on_device(
    n_req,
    n_x,
    hidden_in,
    ln_gain,
    ln_bias,
    w_qkv,
    b_qkv,
    w_out,
    b_out,
    alibi_slope,
    prefix_k,
    prefix_v,
    suffix_len,
    group_of,
    block_of_device,
):
    _, slots, width = hidden_in.shape
    heads = alibi_slope.shape[0]
    size = w_qkv.shape[2] // heads
    block = prefix_k.shape[0]
    n_rc = slots // ROWS
    n_z = n_req // n_x
    smem = pl.BlockSpec(memory_space=pltpu.SMEM)
    anywhere = pl.BlockSpec(memory_space=pl.ANY)
    dma = pltpu.SemaphoreType.DMA
    cache = jax.ShapeDtypeStruct((1, slots, width), BF16)
    held = pltpu.VMEM((1, slots, width), BF16)
    fast = pl.BlockSpec(memory_space=pltpu.VMEM)
    results = pl.pallas_call(
        functools.partial(kernel, n_req, n_x, heads),
        out_shape=(held, held, held),
        in_specs=[smem] * 4 + [anywhere] * 9,
        out_specs=(fast, fast, fast),
        scratch_shapes=[
            pltpu.VMEM((4, slots, width), BF16),
            pltpu.VMEM(w_qkv.shape, BF16),
            pltpu.VMEM((4, w_out.shape[0], width), BF16),
            pltpu.VMEM((w_out.shape[0] // 4, width), BF16),
            pltpu.VMEM((ROWS, 4 * width), BF16),
            pltpu.VMEM((3, heads, slots, size), BF16),
            pltpu.VMEM((4, heads, slots, size), BF16),
            pltpu.VMEM((ROWS, width), F32),
            pltpu.VMEM((1, 4 * width), F32),
            pltpu.VMEM((1, 4 * width), F32),
            pltpu.VMEM((3, width), F32),
            pltpu.VMEM((4, 1, width), F32),
            pltpu.VMEM((n_req, 8, 128), jnp.int32),
            pltpu.VMEM((8, 128), jnp.int32),
        ]
        + [pltpu.VMEM((n_req, 2, block, size), BF16) for _ in range(heads)]
        + [
            dma((7,)),
            dma((heads, 2)),
            dma((3, n_rc)),
            dma((3, n_rc)),
            dma((2, heads, n_z)),
            dma((n_x - 1, heads, n_z)),
            dma((n_x - 1, heads)),
            dma((heads, n_req)),
            dma((3, heads, n_rc)),
            dma((3, heads, n_rc)),
            dma((4,)),
            dma((4,)),
            dma((6,)),
            dma((6,)),
            dma((n_req,)),
            dma((n_req,)),
        ],
        compiler_params=pltpu.CompilerParams(
            collective_id=0, has_side_effects=True, vmem_limit_bytes=58 << 20
        ),
        name="sublayer",
    )(
        block_of_device,
        group_of,
        suffix_len,
        alibi_slope,
        hidden_in,
        ln_gain[None],
        ln_bias[None],
        w_qkv,
        b_qkv,
        w_out,
        b_out.reshape(4, 1, width),
        prefix_k,
        prefix_v,
    )
    return pl.pallas_call(
        land,
        out_shape=(cache, cache, cache),
        in_specs=[anywhere] * 3,
        out_specs=(anywhere,) * 3,
        scratch_shapes=[dma((3,))],
        compiler_params=pltpu.CompilerParams(vmem_limit_bytes=1 << 20),
        name="land",
    )(*(pltpu.with_memory_space_constraint(a, pltpu.VMEM) for a in results))


def solution(mesh):
    n_req = mesh.shape["req"]
    n_x = 2 if n_req <= 8 else 4
    return jax.shard_map(
        functools.partial(on_device, n_req, n_x),
        mesh=mesh,
        in_specs=(
            P("req", None, "tp"),
            P(),
            P(),
            P(None, None, "tp"),
            P(None, "tp"),
            P("tp", None),
            P(),
            P("tp"),
            P("req", "tp"),
            P("req", "tp"),
            P("req"),
            P("req"),
            P("req"),
        ),
        out_specs=(P("req", None, "tp"), P("req", None, "tp"), P("req", None, "tp")),
        check_vma=False,
    )
```

```python
import functools
import math

import jax
import jax.numpy as jnp
from jax import lax
from jax.experimental import pallas as pl
from jax.experimental.pallas import tpu as pltpu
from jax.sharding import PartitionSpec as P

EPS = 1e-05
NEGATIVE = -1e30
LOG2E = math.log2(math.e)
ROWS = 256
STEP = 4
F32 = jnp.float32
BF16 = jnp.bfloat16


def dot_t(a, b):
    return lax.dot_general(a, b, (((1,), (1,)), ((), ())), preferred_element_type=F32)


PLAN = (
    ("own", 0), ("own", 1), ("hidden", 0), ("below", 0, 1), ("hidden", 1), ("hidden", 2), ("hidden", 3),
    ("above", 0, 1), ("weights",), ("own", 2), ("below", 0, 2), ("above", 0, 2), ("own", 3), ("below", 1, 1),
    ("project", 0), ("below", 0, 3), ("below", 2, 1), ("above", 0, 3), ("above", 2, 1), ("above", 1, 1),
    ("project", 1), ("names",), ("attend", 0, 1), ("attend", 0, 0), ("below", 2, 2), ("below", 1, 2),
    ("above", 2, 2), ("above", 3, 1), ("above", 1, 2), ("project", 2), ("below", 3, 1), ("attend", 0, 2),
    ("below", 2, 3), ("above", 2, 3), ("peer", 1), ("above", 3, 2), ("below", 1, 3), ("project", 3),
    ("attend", 0, 3), ("below", 3, 2), ("w1",), ("above", 1, 3), ("peer", 3), ("attend", 2, 1),
    ("attend", 2, 2), ("attend", 2, 3), ("below", 3, 3), ("above", 3, 3), ("w2",), ("attend", 2, 0),
    ("attend", 1, 0), ("attend", 1, 2), ("attend", 1, 3), ("attend", 1, 1), ("attend", 3, 1),
    ("attend", 3, 0), ("w3",), ("attend", 3, 2), ("w4",), ("attend", 3, 3),
)
HALVED = (1, 3)
NAMED = 0


def plan(heads, n_rc, n_z):
    if (heads, n_rc, n_z) == (4, 4, 4):
        return PLAN
    steps = [("hidden", i) for i in range(n_rc)] + [("weights",)]
    for k in range(heads + n_z - 1):
        for h in range(heads):
            s = k - h
            if s == 0:
                steps.append(("own", h))
            elif 0 < s < n_z:
                steps += [("below", h, s), ("above", h, s)]
                if s == 1 and h in HALVED:
                    steps.append(("peer", h))
        if 0 < k <= n_rc:
            steps.append(("project", k - 1))
    steps += [("names",), ("w1",), ("w2",), ("w3",), ("w4",)]
    return steps + [("attend", h, i) for h in range(heads) for i in range(n_rc)]


def kernel(n_req, n_x, heads, *refs):
    (block_ref, group_ref, length_ref, slope_in, hid, gain_in, beta_in, w_qkv, b_qkv_in, w_out, b_out_in, pk, pv) = refs[:13]
    mixed, ck, cv = refs[13:16]
    (hbuf, wq, wcol, wst, nrm, qkv, att, acc, gain, beta, b_qkv, b_out, ids, slope, holds) = refs[16:31]
    kvh = refs[31 : 31 + heads]
    (loc, kvl, hs, hr, zs, xs, es, kvr, as_, ar, wy_s, wy_r, wq_s, wq_r, ids_send, ids_recv) = refs[31 + heads :]

    slots, width = hid.shape[1], hid.shape[2]
    block = pk.shape[0]
    size = width // heads
    n_rc = slots // ROWS
    n_z = n_req // n_x
    nb = n_req // 2
    prefix = nb * block
    feats = 4 * width
    quarter = width // 4

    r = lax.axis_index("req")
    t = lax.axis_index("tp")
    y, c = t // 2, t % 2
    sib = y * 2 + (1 - c)
    oth = (1 - y) * 2 + c
    far = (1 - y) * 2 + (1 - c)
    z, x = r // n_x, r % n_x
    x_peers = [z * n_x + (x + d) % n_x for d in range(1, n_x)]
    z_even = z % 2 == 0
    z_pair = r + n_x - 2 * n_x * (z % 2)
    x_pair = r + 1 - 2 * (x % 2)
    quad = (z % 2) * 2 + x % 2
    quad_z = (1 - z % 2) * 2 + x % 2
    quad_x = (z % 2) * 2 + 1 - x % 2
    quad_d = (1 - z % 2) * 2 + 1 - x % 2

    def remote(src, dst, send, recv, dev):
        return pltpu.make_async_remote_copy(
            src_ref=src,
            dst_ref=dst,
            send_sem=send,
            recv_sem=recv,
            device_id=dev,
            device_id_type=pl.DeviceIdType.MESH,
        )

    def launch(copies):
        for copy in copies:
            copy.start()

    def sent(copies):
        for copy in copies:
            copy.wait_send()

    def arrived(dst, recv):
        remote(dst, dst, loc.at[0], recv, (r, sib)).wait_recv()

    def rows_of(i):
        return pl.ds(pl.multiple_of(i * ROWS, ROWS), ROWS)

    def cols_of(k):
        return pl.ds(pl.multiple_of(k * width, width), width)

    def quarter_of(q):
        return pl.ds(pl.multiple_of(q * quarter, quarter), quarter)

    barrier = pltpu.get_barrier_semaphore()

    def greet(dev):
        pl.semaphore_signal(barrier, inc=1, device_id=dev, device_id_type=pl.DeviceIdType.MESH)

    greet((r, sib))
    greet((r, oth))

    for peer in x_peers:
        greet((peer, t))

    @pl.when(z > 0)
    def _():
        greet((r - n_x, t))

    @pl.when(z < n_z - 1)
    def _():
        greet((r + n_x, t))

    def own_kv(h, a):
        cols = slice(h * size, (h + 1) * size)
        return pltpu.make_async_copy((pk, pv)[a].at[:, cols], kvh[h].at[r, a], kvl.at[h, a])

    own = [
        pltpu.make_async_copy(hid.at[0], hbuf.at[t], loc.at[0]),
        pltpu.make_async_copy(w_qkv, wq, loc.at[1]),
        pltpu.make_async_copy(w_out.at[:, cols_of(t)], wcol.at[t], loc.at[2]),
        pltpu.make_async_copy(gain_in, gain, loc.at[3]),
        pltpu.make_async_copy(beta_in, beta, loc.at[4]),
        pltpu.make_async_copy(b_qkv_in, b_qkv, loc.at[5]),
        pltpu.make_async_copy(b_out_in, b_out, loc.at[6]),
        pltpu.make_async_copy(slope_in, slope, loc.at[7]),
    ]
    for a in range(2):
        own_kv(0, a).start()
    for h in range(1, heads):
        for a in range(2):
            own_kv(h, a).start()
    for copy in own:
        copy.start()
    ids[r] = jnp.full(ids.shape[1:], block_ref[0], jnp.int32)
    ends = jnp.where(z > 0, 1, 0) + jnp.where(z < n_z - 1, 1, 0)
    pl.semaphore_wait(barrier, 1 + n_x + ends)

    def h_other(i):
        rows = rows_of(i)
        return remote(hid.at[0, rows], hbuf.at[t, rows], hs.at[0, i], hr.at[0, i], (r, oth))

    def h_sib(i):
        rows = rows_of(i)
        return remote(hid.at[0, rows], hbuf.at[t, rows], hs.at[1, i], hr.at[1, i], (r, sib))

    def h_fwd(i):
        rows = rows_of(i)
        return remote(hbuf.at[oth, rows], hbuf.at[oth, rows], hs.at[2, i], hr.at[2, i], (r, sib))

    def w_sib():
        return remote(w_out.at[:, cols_of(sib)], wcol.at[t], wy_s.at[0], wy_r.at[0], (r, sib))

    def w_oth():
        rows = quarter_of(quad)
        return remote(w_out.at[rows, cols_of(oth)], wcol.at[t, rows], wy_s.at[1], wy_r.at[1], (r, oth))

    def w_far():
        rows = quarter_of(quad)
        return remote(w_out.at[rows, cols_of(far)], wst, wy_s.at[2], wy_r.at[2], (r, oth))

    def w_fwd():
        return remote(wst, wcol.at[oth, quarter_of(quad)], wy_s.at[3], wy_r.at[3], (r, sib))

    def w_piece(g, q, k, dev):
        here = wcol.at[(oth, far)[g], quarter_of(q)]
        return remote(here, here, wq_s.at[k], wq_r.at[k], (dev, t))

    def w_spread():
        return [w_piece(g, quad, k * 2 + g, (z_pair, x_pair)[k]) for k in range(2) for g in range(2)]

    def w_last(k):
        return w_piece(k, (quad_x, quad_z)[k], 4 + k, (z_pair, x_pair)[k])

    def pieces(h, zj, send, dev):
        j = zj * n_x + x
        here = kvh[h].at[j]
        out = [remote(here, here, send[0].at[send[1], h, zj], kvr.at[h, j], dev)]
        if h == NAMED:
            out.append(remote(ids.at[j], ids.at[j], ids_send.at[send[2], zj], ids_recv.at[j], dev))
        return out

    def up(h, zj):
        return pieces(h, zj, (zs, 0, 0), (r + n_x, t))

    def down(h, zj):
        return pieces(h, zj, (zs, 1, 1), (r - n_x, t))

    def across(h, zj, d):
        return pieces(h, zj, (xs, d, 2 + d), (x_peers[d], t))

    def extra(h, d):
        here = kvh[h].at[x_peers[d]]
        return remote(here, here, es.at[d, h], kvr.at[h, x_peers[d]], (z_pair, t))

    def kv_wait(h, j):
        arrived(kvh[h].at[j], kvr.at[h, j])

    def name_wait(h, j):
        if h == NAMED:
            arrived(ids.at[j], ids_recv.at[j])

    def send_own(h):
        for a in range(2):
            own_kv(h, a).wait()

        @pl.when(z < n_z - 1)
        def _():
            launch(up(h, z))

        @pl.when(z > 0)
        def _():
            launch(down(h, z))

        for d in range(n_x - 1):
            launch(across(h, z, d))

    def from_below(h, s):
        @pl.when(z - s >= 0)
        def _():
            zj = z - s
            kv_wait(h, zj * n_x + x)
            name_wait(h, zj * n_x + x)

            @pl.when(z < n_z - 1)
            def _():
                launch(up(h, zj))

            spread(h, s, zj, z_even)

    def from_above(h, s):
        @pl.when(z + s < n_z)
        def _():
            zj = z + s
            kv_wait(h, zj * n_x + x)
            name_wait(h, zj * n_x + x)

            @pl.when(z > 0)
            def _():
                launch(down(h, zj))

            spread(h, s, zj, jnp.logical_not(z_even))

    def spread(h, s, zj, whole):
        def go():
            for d in range(n_x - 1):
                launch(across(h, zj, d))

        if h in HALVED and s == 1:
            pl.when(whole)(go)
        else:
            go()

    def pass_peer(h):
        for d in range(n_x - 1):
            kv_wait(h, x_peers[d])
            extra(h, d).start()

    def kv_rest(h):
        def one(zj, carry):
            def wait():
                for d in range(1, n_x):
                    kv_wait(h, zj * n_x + (x + d) % n_x)

            if h in HALVED:
                pl.when(zj != z)(wait)
            else:
                wait()
            return carry

        lax.fori_loop(0, n_z, one, 0)

    def live(i):
        slot = lax.broadcasted_iota(jnp.int32, (ROWS, width), 0) + i * ROWS
        return slot < length_ref[0]

    def project(i):
        rows = rows_of(i)
        h_other(i).wait_recv()
        h_fwd(i).start()
        h_sib(i).wait_recv()
        h_fwd(i).wait_recv()
        pieces = [hbuf[f, rows, :].astype(F32) for f in range(4)]
        mean = sum(jnp.sum(p, axis=1, keepdims=True) for p in pieces) * (1.0 / feats)
        pieces = [p - mean for p in pieces]
        var = sum(jnp.sum(p * p, axis=1, keepdims=True) for p in pieces) * (1.0 / feats)
        inv = 1.0 / jnp.sqrt(var + EPS)
        for f in range(4):
            cols = slice(f * width, (f + 1) * width)
            nrm[:, cols] = (pieces[f] * inv * gain[:, cols] + beta[:, cols]).astype(BF16)
        keep = live(i)
        for j in range(3):
            out = jnp.dot(nrm[...], wq[j], preferred_element_type=F32) + b_qkv[j : j + 1, :]
            out = out.astype(BF16)
            for h in range(heads):
                qkv[j, h, rows, :] = out[:, h * size : (h + 1) * size]
            if j > 0:
                (ck, cv)[j - 1][0, rows, :] = jnp.where(keep, out, jnp.zeros_like(out))

    scale2 = LOG2E / math.sqrt(size)
    tri = lax.broadcasted_iota(jnp.int32, (ROWS, ROWS), 1) <= lax.broadcasted_iota(
        jnp.int32, (ROWS, ROWS), 0
    )
    slot_ids = lax.broadcasted_iota(jnp.int32, (1, slots), 1)
    block_ids = lax.broadcasted_iota(jnp.int32, (1, block), 1)

    def a_other(h, i):
        here = att.at[t, h, rows_of(i)]
        return remote(here, here, as_.at[0, h, i], ar.at[0, h, i], (r, oth))

    def a_sib(h, i):
        here = att.at[t, h, rows_of(i)]
        return remote(here, here, as_.at[1, h, i], ar.at[1, h, i], (r, sib))

    def a_fwd(h, i):
        here = att.at[oth, h, rows_of(i)]
        return remote(here, here, as_.at[2, h, i], ar.at[2, h, i], (r, sib))

    def attend(h, i):
        lo, hi = i * ROWS, (i + 1) * ROWS
        slope2 = slope[h] * LOG2E
        q = qkv[0, h, lo:hi, :]
        shift = jnp.where(slot_ids < length_ref[0], slot_ids.astype(F32) * slope2, NEGATIVE)
        sd = dot_t(q, qkv[1, h, lo:hi, :]) * scale2 + shift[:, lo:hi]
        scores = [(jnp.where(tri, sd, NEGATIVE), lambda: qkv[2, h, lo:hi, :])]
        if i > 0:
            so = dot_t(q, qkv[1, h, 0:lo, :]) * scale2 + shift[:, 0:lo]
            scores.append((so, lambda: qkv[2, h, 0:lo, :]))

        def part(p, j):
            place = (block_ids + (p * block - prefix)).astype(F32) * slope2
            return dot_t(q, kvh[h][j, 0]) * scale2 + place, lambda: kvh[h][j, 1]

        def fold(scores, state):
            m = state[0] if state else None
            for s, _ in scores:
                top = jnp.max(s, axis=1, keepdims=True)
                m = top if m is None else jnp.maximum(m, top)
            total = out = None
            if state:
                fac = jnp.exp2(state[0] - m)
                total, out = state[1] * fac, state[2] * fac
            for s, values in scores:
                w = jnp.exp2(s - m)
                sums = jnp.sum(w, axis=1, keepdims=True)
                prod = jnp.dot(w.astype(BF16), values(), preferred_element_type=F32)
                total = sums if total is None else total + sums
                out = prod if out is None else out + prod
            return m, total, out

        def more(g, state):
            return fold([part(g * STEP + k, holds[g * STEP + k]) for k in range(STEP)], state)

        state = fold(scores + [part(k, holds[k]) for k in range(STEP)], None)
        if nb > STEP:
            state = lax.fori_loop(1, nb // STEP, more, state)
        att[t, h, lo:hi, :] = (state[2] / state[1]).astype(BF16)
        a_other(h, i).start()
        a_sib(h, i).start()

    def weights_first():
        arrived(wst, wy_r.at[2])
        w_fwd().start()

    def weights_spread():
        here = quarter_of(quad)
        arrived(wcol.at[oth, here], wy_r.at[1])
        arrived(wcol.at[far, here], wy_r.at[3])
        for copy in w_spread():
            copy.start()

    def weights_third():
        arrived(wcol.at[oth, quarter_of(quad_x)], wq_r.at[2])
        w_last(0).start()

    def weights_fourth():
        arrived(wcol.at[far, quarter_of(quad_z)], wq_r.at[1])
        w_last(1).start()

    def weights_rest():
        own[2].wait()
        arrived(wcol.at[sib], wy_r.at[0])
        arrived(wcol.at[oth, quarter_of(quad_z)], wq_r.at[0])
        arrived(wcol.at[far, quarter_of(quad_x)], wq_r.at[3])
        arrived(wcol.at[oth, quarter_of(quad_d)], wq_r.at[4])
        arrived(wcol.at[far, quarter_of(quad_d)], wq_r.at[5])

    def hidden_send(i):
        h_other(i).start()
        h_sib(i).start()

    def weights_send():
        w_oth().start()
        w_far().start()
        w_sib().start()

    def names():
        def one(zj, carry):
            for d in range(1, n_x):
                name_wait(NAMED, zj * n_x + (x + d) % n_x)
            return carry

        lax.fori_loop(0, n_z, one, 0)
        for p in range(nb):
            found = jnp.zeros(ids.shape[1:], jnp.int32)
            for j in range(n_req):
                found = jnp.maximum(found, jnp.where(ids[j] == group_ref[0] * nb + p, j, 0))
            holds[p] = jnp.max(found)

    begun = set()

    def attend_unit(h, i):
        if h not in begun:
            begun.add(h)
            kv_rest(h)
        attend(h, i)

    do = {
        "hidden": hidden_send,
        "weights": weights_send,
        "own": send_own,
        "below": from_below,
        "above": from_above,
        "peer": pass_peer,
        "names": names,
        "w1": weights_first,
        "w2": weights_spread,
        "w3": weights_third,
        "w4": weights_fourth,
        "attend": attend_unit,
    }
    groups = [[]]
    for step in plan(heads, n_rc, n_z):
        if step[0] == "project":
            groups.append([])
        else:
            groups[-1].append(step)

    def run(steps):
        for step in steps:
            do[step[0]](*step[1:])

    run(groups[0])
    own[0].wait()
    for copy in own[3:]:
        copy.wait()
    own[1].wait()

    def prepare(i, carry):
        project(i)
        for k in range(n_rc - 1):
            if groups[k + 1]:

                @pl.when(i == k)
                def _(k=k):
                    run(groups[k + 1])

        return carry

    lax.fori_loop(0, n_rc, prepare, 0)
    run(groups[n_rc])

    def a_take(h, i):
        arrived(att.at[oth, h, rows_of(i)], ar.at[0, h, i])
        a_fwd(h, i).start()

    def drain_first(i, carry):
        h_other(i).wait_send()
        h_sib(i).wait_send()
        h_fwd(i).wait_send()
        return carry

    def drain_att(heads_, i):
        for h in heads_:
            a_other(h, i).wait_send()
            a_sib(h, i).wait_send()
            a_fwd(h, i).wait_send()

    def drain_most(i, carry):
        drain_att(range(heads - 1), i)
        return carry

    def drain_last(i, carry):
        drain_att([heads - 1], i)
        return carry

    lax.fori_loop(0, n_rc, drain_first, 0)

    def drain_prefix(zj, carry):
        for h in range(heads):

            @pl.when(jnp.logical_and(zj <= z, z < n_z - 1))
            def _(h=h):
                sent(up(h, zj))

            @pl.when(jnp.logical_and(zj >= z, z > 0))
            def _(h=h):
                sent(down(h, zj))

            def waits(h=h):
                for d in range(n_x - 1):
                    sent(across(h, zj, d))

            if h in HALVED:
                pl.when(zj != z + 1 - 2 * (z % 2))(waits)
            else:
                waits()
        return carry

    lax.fori_loop(0, n_z, drain_prefix, 0)
    for h in HALVED:
        for d in range(n_x - 1):
            extra(h, d).wait_send()

    for h in range(heads - 1):

        def take(i, carry, h=h):
            a_take(h, i)
            return carry

        lax.fori_loop(0, n_rc, take, 0)
    weights_rest()

    lax.fori_loop(0, n_rc, drain_most, 0)
    for copy in [w_sib(), w_oth(), w_far(), w_fwd()] + w_spread() + [w_last(0), w_last(1)]:
        copy.wait_send()

    a_take(heads - 1, 0)

    def final(i, carry):
        rows = rows_of(i)

        def term(f):
            lhs = jnp.concatenate([att[f, h, rows, :] for h in range(heads)], axis=1)
            return jnp.dot(lhs, wcol[f], preferred_element_type=F32)

        for h in range(heads):
            arrived(att.at[sib, h, rows], ar.at[1, h, i])
        acc[...] = term(t) + term(sib) + term(oth) + b_out[t] + hbuf[t, rows, :].astype(F32)

        @pl.when(i + 1 < n_rc)
        def _():
            a_take(heads - 1, i + 1)

        for h in range(heads):
            arrived(att.at[far, h, rows], ar.at[2, h, i])
        out = acc[...] + term(far)
        mixed[0, rows, :] = jnp.where(live(i), out, 0.0).astype(BF16)
        return carry

    lax.fori_loop(0, n_rc, final, 0)

    lax.fori_loop(0, n_rc, drain_last, 0)


def land(*refs):
    copies = [pltpu.make_async_copy(refs[k], refs[k + 3], refs[6].at[k]) for k in range(3)]
    for copy in copies:
        copy.start()
    for copy in copies:
        copy.wait()


def on_device(
    n_req,
    n_x,
    hidden_in,
    ln_gain,
    ln_bias,
    w_qkv,
    b_qkv,
    w_out,
    b_out,
    alibi_slope,
    prefix_k,
    prefix_v,
    suffix_len,
    group_of,
    block_of_device,
):
    _, slots, width = hidden_in.shape
    heads = alibi_slope.shape[0]
    size = w_qkv.shape[2] // heads
    block = prefix_k.shape[0]
    n_rc = slots // ROWS
    n_z = n_req // n_x
    smem = pl.BlockSpec(memory_space=pltpu.SMEM)
    anywhere = pl.BlockSpec(memory_space=pl.ANY)
    dma = pltpu.SemaphoreType.DMA
    cache = jax.ShapeDtypeStruct((1, slots, width), BF16)
    held = pltpu.VMEM((1, slots, width), BF16)
    fast = pl.BlockSpec(memory_space=pltpu.VMEM)
    results = pl.pallas_call(
        functools.partial(kernel, n_req, n_x, heads),
        out_shape=(held, held, held),
        in_specs=[smem] * 3 + [anywhere] * 10,
        out_specs=(fast, fast, fast),
        scratch_shapes=[
            pltpu.VMEM((4, slots, width), BF16),
            pltpu.VMEM(w_qkv.shape, BF16),
            pltpu.VMEM((4, w_out.shape[0], width), BF16),
            pltpu.VMEM((w_out.shape[0] // 4, width), BF16),
            pltpu.VMEM((ROWS, 4 * width), BF16),
            pltpu.VMEM((3, heads, slots, size), BF16),
            pltpu.VMEM((4, heads, slots, size), BF16),
            pltpu.VMEM((ROWS, width), F32),
            pltpu.VMEM((1, 4 * width), F32),
            pltpu.VMEM((1, 4 * width), F32),
            pltpu.VMEM((3, width), F32),
            pltpu.VMEM((4, 1, width), F32),
            pltpu.VMEM((n_req, 8, 128), jnp.int32),
            pltpu.SMEM((heads,), F32),
            pltpu.SMEM((n_req // 2,), jnp.int32),
        ]
        + [pltpu.VMEM((n_req, 2, block, size), BF16) for _ in range(heads)]
        + [
            dma((8,)),
            dma((heads, 2)),
            dma((3, n_rc)),
            dma((3, n_rc)),
            dma((2, heads, n_z)),
            dma((n_x - 1, heads, n_z)),
            dma((n_x - 1, heads)),
            dma((heads, n_req)),
            dma((3, heads, n_rc)),
            dma((3, heads, n_rc)),
            dma((4,)),
            dma((4,)),
            dma((6,)),
            dma((6,)),
            dma((n_x + 1, n_z)),
            dma((n_req,)),
        ],
        compiler_params=pltpu.CompilerParams(
            collective_id=0, has_side_effects=True, vmem_limit_bytes=58 << 20
        ),
        name="sublayer",
    )(
        block_of_device,
        group_of,
        suffix_len,
        alibi_slope,
        hidden_in,
        ln_gain[None],
        ln_bias[None],
        w_qkv,
        b_qkv,
        w_out,
        b_out.reshape(4, 1, width),
        prefix_k,
        prefix_v,
    )
    return pl.pallas_call(
        land,
        out_shape=(cache, cache, cache),
        in_specs=[anywhere] * 3,
        out_specs=(anywhere,) * 3,
        scratch_shapes=[dma((3,))],
        compiler_params=pltpu.CompilerParams(vmem_limit_bytes=1 << 20),
        name="land",
    )(*(pltpu.with_memory_space_constraint(a, pltpu.VMEM) for a in results))


def solution(mesh):
    n_req = mesh.shape["req"]
    n_x = 2 if n_req <= 8 else 4
    return jax.shard_map(
        functools.partial(on_device, n_req, n_x),
        mesh=mesh,
        in_specs=(
            P("req", None, "tp"),
            P(),
            P(),
            P(None, None, "tp"),
            P(None, "tp"),
            P("tp", None),
            P(),
            P("tp"),
            P("req", "tp"),
            P("req", "tp"),
            P("req"),
            P("req"),
            P("req"),
        ),
        out_specs=(P("req", None, "tp"), P("req", None, "tp"), P("req", None, "tp")),
        check_vma=False,
    )
```

```python
import functools
import math

import jax
import jax.numpy as jnp
from jax import lax
from jax.experimental import pallas as pl
from jax.experimental.pallas import tpu as pltpu
from jax.sharding import PartitionSpec as P

EPS = 1e-05
NEGATIVE = -1e30
LOG2E = math.log2(math.e)
ROWS = 256
STEP = 4
F32 = jnp.float32
BF16 = jnp.bfloat16


def dot_t(a, b):
    return lax.dot_general(a, b, (((1,), (1,)), ((), ())), preferred_element_type=F32)


PLAN = (
    ("own", 0), ("own", 1), ("hidden", 0), ("below", 0, 1), ("hidden", 1), ("hidden", 2), ("hidden", 3),
    ("above", 0, 1), ("weights",), ("own", 2), ("below", 0, 2), ("above", 0, 2), ("own", 3), ("below", 1, 1),
    ("project", 0), ("below", 0, 3), ("below", 2, 1), ("above", 0, 3), ("above", 2, 1), ("above", 1, 1),
    ("project", 1), ("names",), ("attend", 0, 1), ("attend", 0, 0), ("below", 2, 2), ("below", 1, 2),
    ("above", 2, 2), ("above", 3, 1), ("above", 1, 2), ("project", 2), ("below", 3, 1), ("attend", 0, 2),
    ("below", 2, 3), ("above", 2, 3), ("peer", 1), ("above", 3, 2), ("below", 1, 3), ("project", 3),
    ("attend", 0, 3), ("below", 3, 2), ("w1",), ("above", 1, 3), ("peer", 3), ("attend", 2, 1),
    ("attend", 2, 2), ("attend", 2, 3), ("below", 3, 3), ("above", 3, 3), ("w2",), ("attend", 2, 0),
    ("attend", 1, 0), ("attend", 1, 2), ("attend", 1, 3), ("attend", 1, 1), ("attend", 3, 1),
    ("attend", 3, 0), ("w3",), ("attend", 3, 2), ("w4",), ("attend", 3, 3),
)
HALVED = (1, 3)
NAMED = 0


def plan(heads, n_rc, n_z):
    if (heads, n_rc, n_z) == (4, 4, 4):
        return PLAN
    steps = [("hidden", i) for i in range(n_rc)] + [("weights",)]
    for k in range(heads + n_z - 1):
        for h in range(heads):
            s = k - h
            if s == 0:
                steps.append(("own", h))
            elif 0 < s < n_z:
                steps += [("below", h, s), ("above", h, s)]
                if s == 1 and h in HALVED:
                    steps.append(("peer", h))
        if 0 < k <= n_rc:
            steps.append(("project", k - 1))
    steps += [("names",), ("w1",), ("w2",), ("w3",), ("w4",)]
    return steps + [("attend", h, i) for h in range(heads) for i in range(n_rc)]


def kernel(n_req, n_x, heads, *refs):
    (block_ref, group_ref, length_ref, slope_in, hid, gain_in, beta_in, w_qkv, b_qkv_in, w_out, b_out_in, pk, pv) = refs[:13]
    mixed, ck, cv = refs[13:16]
    (hbuf, wq, wcol, wst, nrm, qkv, att, acc, gain, beta, b_qkv, b_out, ids, slope, holds) = refs[16:31]
    kvh = refs[31 : 31 + heads]
    (loc, kvl, hs, hr, zs, xs, es, kvr, as_, ar, wy_s, wy_r, wq_s, wq_r, ids_send, ids_recv) = refs[31 + heads :]

    slots, width = hid.shape[1], hid.shape[2]
    block = pk.shape[0]
    size = width // heads
    n_rc = slots // ROWS
    n_z = n_req // n_x
    nb = n_req // 2
    prefix = nb * block
    feats = 4 * width
    quarter = width // 4

    r = lax.axis_index("req")
    t = lax.axis_index("tp")
    y, c = t // 2, t % 2
    sib = y * 2 + (1 - c)
    oth = (1 - y) * 2 + c
    far = (1 - y) * 2 + (1 - c)
    z, x = r // n_x, r % n_x
    x_peers = [z * n_x + (x + d) % n_x for d in range(1, n_x)]
    z_even = z % 2 == 0
    z_pair = r + n_x - 2 * n_x * (z % 2)
    x_pair = r + 1 - 2 * (x % 2)
    quad = (z % 2) * 2 + x % 2
    quad_z = (1 - z % 2) * 2 + x % 2
    quad_x = (z % 2) * 2 + 1 - x % 2
    quad_d = (1 - z % 2) * 2 + 1 - x % 2

    def remote(src, dst, send, recv, dev):
        return pltpu.make_async_remote_copy(
            src_ref=src,
            dst_ref=dst,
            send_sem=send,
            recv_sem=recv,
            device_id=dev,
            device_id_type=pl.DeviceIdType.MESH,
        )

    def launch(copies):
        for copy in copies:
            copy.start()

    def sent(copies):
        for copy in copies:
            copy.wait_send()

    def arrived(dst, recv):
        remote(dst, dst, loc.at[0], recv, (r, sib)).wait_recv()

    def rows_of(i):
        return pl.ds(pl.multiple_of(i * ROWS, ROWS), ROWS)

    def cols_of(k):
        return pl.ds(pl.multiple_of(k * width, width), width)

    def quarter_of(q):
        return pl.ds(pl.multiple_of(q * quarter, quarter), quarter)

    barrier = pltpu.get_barrier_semaphore()

    def greet(dev):
        pl.semaphore_signal(barrier, inc=1, device_id=dev, device_id_type=pl.DeviceIdType.MESH)

    greet((r, sib))
    greet((r, oth))

    for peer in x_peers:
        greet((peer, t))

    @pl.when(z > 0)
    def _():
        greet((r - n_x, t))

    @pl.when(z < n_z - 1)
    def _():
        greet((r + n_x, t))

    def own_kv(h, a):
        cols = slice(h * size, (h + 1) * size)
        return pltpu.make_async_copy((pk, pv)[a].at[:, cols], kvh[h].at[r, a], kvl.at[h, a])

    own = [
        pltpu.make_async_copy(hid.at[0], hbuf.at[t], loc.at[0]),
        pltpu.make_async_copy(w_qkv, wq, loc.at[1]),
        pltpu.make_async_copy(w_out.at[:, cols_of(t)], wcol.at[t], loc.at[2]),
        pltpu.make_async_copy(gain_in, gain, loc.at[3]),
        pltpu.make_async_copy(beta_in, beta, loc.at[4]),
        pltpu.make_async_copy(b_qkv_in, b_qkv, loc.at[5]),
        pltpu.make_async_copy(b_out_in, b_out, loc.at[6]),
        pltpu.make_async_copy(slope_in, slope, loc.at[7]),
    ]
    for a in range(2):
        own_kv(0, a).start()
    for h in range(1, heads):
        for a in range(2):
            own_kv(h, a).start()
    ids[r] = jnp.full(ids.shape[1:], block_ref[0], jnp.int32)
    ends = jnp.where(z > 0, 1, 0) + jnp.where(z < n_z - 1, 1, 0)
    pl.semaphore_wait(barrier, 1 + n_x + ends)

    def h_other(i):
        rows = rows_of(i)
        return remote(hid.at[0, rows], hbuf.at[t, rows], hs.at[0, i], hr.at[0, i], (r, oth))

    def h_sib(i):
        rows = rows_of(i)
        return remote(hid.at[0, rows], hbuf.at[t, rows], hs.at[1, i], hr.at[1, i], (r, sib))

    def h_fwd(i):
        rows = rows_of(i)
        return remote(hbuf.at[oth, rows], hbuf.at[oth, rows], hs.at[2, i], hr.at[2, i], (r, sib))

    def w_sib():
        return remote(w_out.at[:, cols_of(sib)], wcol.at[t], wy_s.at[0], wy_r.at[0], (r, sib))

    def w_oth():
        rows = quarter_of(quad)
        return remote(w_out.at[rows, cols_of(oth)], wcol.at[t, rows], wy_s.at[1], wy_r.at[1], (r, oth))

    def w_far():
        rows = quarter_of(quad)
        return remote(w_out.at[rows, cols_of(far)], wst, wy_s.at[2], wy_r.at[2], (r, oth))

    def w_fwd():
        return remote(wst, wcol.at[oth, quarter_of(quad)], wy_s.at[3], wy_r.at[3], (r, sib))

    def w_piece(g, q, k, dev):
        here = wcol.at[(oth, far)[g], quarter_of(q)]
        return remote(here, here, wq_s.at[k], wq_r.at[k], (dev, t))

    def w_spread():
        return [w_piece(g, quad, k * 2 + g, (z_pair, x_pair)[k]) for k in range(2) for g in range(2)]

    def w_last(k):
        return w_piece(k, (quad_x, quad_z)[k], 4 + k, (z_pair, x_pair)[k])

    def pieces(h, zj, send, dev):
        j = zj * n_x + x
        here = kvh[h].at[j]
        out = [remote(here, here, send[0].at[send[1], h, zj], kvr.at[h, j], dev)]
        if h == NAMED:
            out.append(remote(ids.at[j], ids.at[j], ids_send.at[send[2], zj], ids_recv.at[j], dev))
        return out

    def up(h, zj):
        return pieces(h, zj, (zs, 0, 0), (r + n_x, t))

    def down(h, zj):
        return pieces(h, zj, (zs, 1, 1), (r - n_x, t))

    def across(h, zj, d):
        return pieces(h, zj, (xs, d, 2 + d), (x_peers[d], t))

    def extra(h, d):
        here = kvh[h].at[x_peers[d]]
        return remote(here, here, es.at[d, h], kvr.at[h, x_peers[d]], (z_pair, t))

    def kv_wait(h, j):
        arrived(kvh[h].at[j], kvr.at[h, j])

    def name_wait(h, j):
        if h == NAMED:
            arrived(ids.at[j], ids_recv.at[j])

    def send_own(h):
        for a in range(2):
            own_kv(h, a).wait()

        @pl.when(z < n_z - 1)
        def _():
            launch(up(h, z))

        @pl.when(z > 0)
        def _():
            launch(down(h, z))

        for d in range(n_x - 1):
            launch(across(h, z, d))

    def from_below(h, s):
        @pl.when(z - s >= 0)
        def _():
            zj = z - s
            kv_wait(h, zj * n_x + x)
            name_wait(h, zj * n_x + x)

            @pl.when(z < n_z - 1)
            def _():
                launch(up(h, zj))

            spread(h, s, zj, z_even)

    def from_above(h, s):
        @pl.when(z + s < n_z)
        def _():
            zj = z + s
            kv_wait(h, zj * n_x + x)
            name_wait(h, zj * n_x + x)

            @pl.when(z > 0)
            def _():
                launch(down(h, zj))

            spread(h, s, zj, jnp.logical_not(z_even))

    def spread(h, s, zj, whole):
        def go():
            for d in range(n_x - 1):
                launch(across(h, zj, d))

        if h in HALVED and s == 1:
            pl.when(whole)(go)
        else:
            go()

    def pass_peer(h):
        for d in range(n_x - 1):
            kv_wait(h, x_peers[d])
            extra(h, d).start()

    def kv_rest(h):
        def one(zj, carry):
            def wait():
                for d in range(1, n_x):
                    kv_wait(h, zj * n_x + (x + d) % n_x)

            if h in HALVED:
                pl.when(zj != z)(wait)
            else:
                wait()
            return carry

        lax.fori_loop(0, n_z, one, 0)

    def live(i):
        slot = lax.broadcasted_iota(jnp.int32, (ROWS, width), 0) + i * ROWS
        return slot < length_ref[0]

    def project(i):
        rows = rows_of(i)
        h_other(i).wait_recv()
        h_fwd(i).start()
        h_sib(i).wait_recv()
        h_fwd(i).wait_recv()
        pieces = [hbuf[f, rows, :].astype(F32) for f in range(4)]
        mean = sum(jnp.sum(p, axis=1, keepdims=True) for p in pieces) * (1.0 / feats)
        pieces = [p - mean for p in pieces]
        var = sum(jnp.sum(p * p, axis=1, keepdims=True) for p in pieces) * (1.0 / feats)
        inv = 1.0 / jnp.sqrt(var + EPS)
        for f in range(4):
            cols = slice(f * width, (f + 1) * width)
            nrm[:, cols] = (pieces[f] * inv * gain[:, cols] + beta[:, cols]).astype(BF16)
        keep = live(i)
        for j in range(3):
            out = jnp.dot(nrm[...], wq[j], preferred_element_type=F32) + b_qkv[j : j + 1, :]
            out = out.astype(BF16)
            for h in range(heads):
                qkv[j, h, rows, :] = out[:, h * size : (h + 1) * size]
            if j > 0:
                (ck, cv)[j - 1][0, rows, :] = jnp.where(keep, out, jnp.zeros_like(out))

    scale2 = LOG2E / math.sqrt(size)
    tri = lax.broadcasted_iota(jnp.int32, (ROWS, ROWS), 1) <= lax.broadcasted_iota(
        jnp.int32, (ROWS, ROWS), 0
    )
    slot_ids = lax.broadcasted_iota(jnp.int32, (1, slots), 1)
    block_ids = lax.broadcasted_iota(jnp.int32, (1, block), 1)

    def a_other(h, i):
        here = att.at[t, h, rows_of(i)]
        return remote(here, here, as_.at[0, h, i], ar.at[0, h, i], (r, oth))

    def a_sib(h, i):
        here = att.at[t, h, rows_of(i)]
        return remote(here, here, as_.at[1, h, i], ar.at[1, h, i], (r, sib))

    def a_fwd(h, i):
        here = att.at[oth, h, rows_of(i)]
        return remote(here, here, as_.at[2, h, i], ar.at[2, h, i], (r, sib))

    def attend(h, i):
        lo, hi = i * ROWS, (i + 1) * ROWS
        slope2 = slope[h] * LOG2E
        q = qkv[0, h, lo:hi, :]
        shift = jnp.where(slot_ids < length_ref[0], slot_ids.astype(F32) * slope2, NEGATIVE)
        sd = dot_t(q, qkv[1, h, lo:hi, :]) * scale2 + shift[:, lo:hi]
        scores = [(jnp.where(tri, sd, NEGATIVE), lambda: qkv[2, h, lo:hi, :])]
        if i > 0:
            so = dot_t(q, qkv[1, h, 0:lo, :]) * scale2 + shift[:, 0:lo]
            scores.append((so, lambda: qkv[2, h, 0:lo, :]))

        def part(p, j):
            place = (block_ids + (p * block - prefix)).astype(F32) * slope2
            return dot_t(q, kvh[h][j, 0]) * scale2 + place, lambda: kvh[h][j, 1]

        def fold(scores, state):
            m = state[0] if state else None
            for s, _ in scores:
                top = jnp.max(s, axis=1, keepdims=True)
                m = top if m is None else jnp.maximum(m, top)
            total = out = None
            if state:
                fac = jnp.exp2(state[0] - m)
                total, out = state[1] * fac, state[2] * fac
            for s, values in scores:
                w = jnp.exp2(s - m)
                sums = jnp.sum(w, axis=1, keepdims=True)
                prod = jnp.dot(w.astype(BF16), values(), preferred_element_type=F32)
                total = sums if total is None else total + sums
                out = prod if out is None else out + prod
            return m, total, out

        def more(g, state):
            return fold([part(g * STEP + k, holds[g * STEP + k]) for k in range(STEP)], state)

        state = fold(scores + [part(k, holds[k]) for k in range(STEP)], None)
        if nb > STEP:
            state = lax.fori_loop(1, nb // STEP, more, state)
        att[t, h, lo:hi, :] = (state[2] / state[1]).astype(BF16)
        a_other(h, i).start()
        a_sib(h, i).start()

    def weights_first():
        arrived(wst, wy_r.at[2])
        w_fwd().start()

    def weights_spread():
        here = quarter_of(quad)
        arrived(wcol.at[oth, here], wy_r.at[1])
        arrived(wcol.at[far, here], wy_r.at[3])
        for copy in w_spread():
            copy.start()

    def weights_third():
        arrived(wcol.at[oth, quarter_of(quad_x)], wq_r.at[2])
        w_last(0).start()

    def weights_fourth():
        arrived(wcol.at[far, quarter_of(quad_z)], wq_r.at[1])
        w_last(1).start()

    def weights_rest():
        own[2].wait()
        arrived(wcol.at[sib], wy_r.at[0])
        arrived(wcol.at[oth, quarter_of(quad_z)], wq_r.at[0])
        arrived(wcol.at[far, quarter_of(quad_x)], wq_r.at[3])
        arrived(wcol.at[oth, quarter_of(quad_d)], wq_r.at[4])
        arrived(wcol.at[far, quarter_of(quad_d)], wq_r.at[5])

    def hidden_send(i):
        h_other(i).start()
        h_sib(i).start()

    def weights_send():
        w_oth().start()
        w_far().start()
        w_sib().start()

    def names():
        def one(zj, carry):
            for d in range(1, n_x):
                name_wait(NAMED, zj * n_x + (x + d) % n_x)
            return carry

        lax.fori_loop(0, n_z, one, 0)
        for p in range(nb):
            found = jnp.zeros(ids.shape[1:], jnp.int32)
            for j in range(n_req):
                found = jnp.maximum(found, jnp.where(ids[j] == group_ref[0] * nb + p, j, 0))
            holds[p] = jnp.max(found)

    begun = set()

    def attend_unit(h, i):
        if h not in begun:
            begun.add(h)
            kv_rest(h)
        attend(h, i)

    do = {
        "hidden": hidden_send,
        "weights": weights_send,
        "own": send_own,
        "below": from_below,
        "above": from_above,
        "peer": pass_peer,
        "names": names,
        "w1": weights_first,
        "w2": weights_spread,
        "w3": weights_third,
        "w4": weights_fourth,
        "attend": attend_unit,
    }
    groups = [[]]
    for step in plan(heads, n_rc, n_z):
        if step[0] == "project":
            groups.append([])
        else:
            groups[-1].append(step)

    def run(steps):
        for step in steps:
            do[step[0]](*step[1:])

    begin = groups[0].index(("hidden", 0))
    run(groups[0][begin : begin + 1] + groups[0][:begin])
    for copy in own:
        copy.start()
    run(groups[0][begin + 1 :])
    own[0].wait()
    for copy in own[3:]:
        copy.wait()
    own[1].wait()

    def prepare(i, carry):
        project(i)
        for k in range(n_rc - 1):
            if groups[k + 1]:

                @pl.when(i == k)
                def _(k=k):
                    run(groups[k + 1])

        return carry

    lax.fori_loop(0, n_rc, prepare, 0)
    run(groups[n_rc])

    def a_take(h, i):
        arrived(att.at[oth, h, rows_of(i)], ar.at[0, h, i])
        a_fwd(h, i).start()

    def drain_first(i, carry):
        h_other(i).wait_send()
        h_sib(i).wait_send()
        h_fwd(i).wait_send()
        return carry

    def drain_att(heads_, i):
        for h in heads_:
            a_other(h, i).wait_send()
            a_sib(h, i).wait_send()
            a_fwd(h, i).wait_send()

    def drain_most(i, carry):
        drain_att(range(heads - 1), i)
        return carry

    def drain_last(i, carry):
        drain_att([heads - 1], i)
        return carry

    lax.fori_loop(0, n_rc, drain_first, 0)

    def drain_prefix(zj, carry):
        for h in range(heads):

            @pl.when(jnp.logical_and(zj <= z, z < n_z - 1))
            def _(h=h):
                sent(up(h, zj))

            @pl.when(jnp.logical_and(zj >= z, z > 0))
            def _(h=h):
                sent(down(h, zj))

            def waits(h=h):
                for d in range(n_x - 1):
                    sent(across(h, zj, d))

            if h in HALVED:
                pl.when(zj != z + 1 - 2 * (z % 2))(waits)
            else:
                waits()
        return carry

    lax.fori_loop(0, n_z, drain_prefix, 0)
    for h in HALVED:
        for d in range(n_x - 1):
            extra(h, d).wait_send()

    for h in range(heads - 1):

        def take(i, carry, h=h):
            a_take(h, i)
            return carry

        lax.fori_loop(0, n_rc, take, 0)
    weights_rest()

    lax.fori_loop(0, n_rc, drain_most, 0)
    for copy in [w_sib(), w_oth(), w_far(), w_fwd()] + w_spread() + [w_last(0), w_last(1)]:
        copy.wait_send()

    a_take(heads - 1, 0)

    def final(i, carry):
        rows = rows_of(i)

        def term(f):
            lhs = jnp.concatenate([att[f, h, rows, :] for h in range(heads)], axis=1)
            return jnp.dot(lhs, wcol[f], preferred_element_type=F32)

        for h in range(heads):
            arrived(att.at[sib, h, rows], ar.at[1, h, i])
        acc[...] = term(t) + term(sib) + term(oth) + b_out[t] + hbuf[t, rows, :].astype(F32)

        @pl.when(i + 1 < n_rc)
        def _():
            a_take(heads - 1, i + 1)

        for h in range(heads):
            arrived(att.at[far, h, rows], ar.at[2, h, i])
        out = acc[...] + term(far)
        mixed[0, rows, :] = jnp.where(live(i), out, 0.0).astype(BF16)
        return carry

    lax.fori_loop(0, n_rc, final, 0)

    lax.fori_loop(0, n_rc, drain_last, 0)


def land(*refs):
    copies = [pltpu.make_async_copy(refs[k], refs[k + 3], refs[6].at[k]) for k in range(3)]
    for copy in copies:
        copy.start()
    for copy in copies:
        copy.wait()


def on_device(
    n_req,
    n_x,
    hidden_in,
    ln_gain,
    ln_bias,
    w_qkv,
    b_qkv,
    w_out,
    b_out,
    alibi_slope,
    prefix_k,
    prefix_v,
    suffix_len,
    group_of,
    block_of_device,
):
    _, slots, width = hidden_in.shape
    heads = alibi_slope.shape[0]
    size = w_qkv.shape[2] // heads
    block = prefix_k.shape[0]
    n_rc = slots // ROWS
    n_z = n_req // n_x
    smem = pl.BlockSpec(memory_space=pltpu.SMEM)
    anywhere = pl.BlockSpec(memory_space=pl.ANY)
    dma = pltpu.SemaphoreType.DMA
    cache = jax.ShapeDtypeStruct((1, slots, width), BF16)
    held = pltpu.VMEM((1, slots, width), BF16)
    fast = pl.BlockSpec(memory_space=pltpu.VMEM)
    results = pl.pallas_call(
        functools.partial(kernel, n_req, n_x, heads),
        out_shape=(held, held, held),
        in_specs=[smem] * 3 + [anywhere] * 10,
        out_specs=(fast, fast, fast),
        scratch_shapes=[
            pltpu.VMEM((4, slots, width), BF16),
            pltpu.VMEM(w_qkv.shape, BF16),
            pltpu.VMEM((4, w_out.shape[0], width), BF16),
            pltpu.VMEM((w_out.shape[0] // 4, width), BF16),
            pltpu.VMEM((ROWS, 4 * width), BF16),
            pltpu.VMEM((3, heads, slots, size), BF16),
            pltpu.VMEM((4, heads, slots, size), BF16),
            pltpu.VMEM((ROWS, width), F32),
            pltpu.VMEM((1, 4 * width), F32),
            pltpu.VMEM((1, 4 * width), F32),
            pltpu.VMEM((3, width), F32),
            pltpu.VMEM((4, 1, width), F32),
            pltpu.VMEM((n_req, 8, 128), jnp.int32),
            pltpu.SMEM((heads,), F32),
            pltpu.SMEM((n_req // 2,), jnp.int32),
        ]
        + [pltpu.VMEM((n_req, 2, block, size), BF16) for _ in range(heads)]
        + [
            dma((8,)),
            dma((heads, 2)),
            dma((3, n_rc)),
            dma((3, n_rc)),
            dma((2, heads, n_z)),
            dma((n_x - 1, heads, n_z)),
            dma((n_x - 1, heads)),
            dma((heads, n_req)),
            dma((3, heads, n_rc)),
            dma((3, heads, n_rc)),
            dma((4,)),
            dma((4,)),
            dma((6,)),
            dma((6,)),
            dma((n_x + 1, n_z)),
            dma((n_req,)),
        ],
        compiler_params=pltpu.CompilerParams(
            collective_id=0, has_side_effects=True, vmem_limit_bytes=58 << 20
        ),
        name="sublayer",
    )(
        block_of_device,
        group_of,
        suffix_len,
        alibi_slope,
        hidden_in,
        ln_gain[None],
        ln_bias[None],
        w_qkv,
        b_qkv,
        w_out,
        b_out.reshape(4, 1, width),
        prefix_k,
        prefix_v,
    )
    return pl.pallas_call(
        land,
        out_shape=(cache, cache, cache),
        in_specs=[anywhere] * 3,
        out_specs=(anywhere,) * 3,
        scratch_shapes=[dma((3,))],
        compiler_params=pltpu.CompilerParams(vmem_limit_bytes=1 << 20),
        name="land",
    )(*(pltpu.with_memory_space_constraint(a, pltpu.VMEM) for a in results))


def solution(mesh):
    n_req = mesh.shape["req"]
    n_x = 2 if n_req <= 8 else 4
    return jax.shard_map(
        functools.partial(on_device, n_req, n_x),
        mesh=mesh,
        in_specs=(
            P("req", None, "tp"),
            P(),
            P(),
            P(None, None, "tp"),
            P(None, "tp"),
            P("tp", None),
            P(),
            P("tp"),
            P("req", "tp"),
            P("req", "tp"),
            P("req"),
            P("req"),
            P("req"),
        ),
        out_specs=(P("req", None, "tp"), P("req", None, "tp"), P("req", None, "tp")),
        check_vma=False,
    )
```
